256 devices in a mesh: hyp: 4 (over z_lo), row: 16 (over x, z_hi, core), col: 4 (over y).
Axes of the slice: x: 4, y: 4, z: 8 (z_hi: 2, z_lo: 4; z = z_hi * 4 + z_lo), core: 2. Of those that a mesh axis runs over, the one named last changes fastest.
Arguments:
- front_orig: bfloat16 [40960, 10240], P(('hyp', 'row'), 'col'), parts along dimension 0, as said below
- child_updates: bfloat16 [65536, 8192], P(('hyp', 'row'), 'col'), parts along dimension 0, as said below
- child_map: int32 [8, 64], P('hyp'), parts along dimension 0, may hold values from 0 to 79, as said below
- panel_inverse: bfloat16 [1024, 256], P('hyp'), parts along dimension 0, as said below
Outputs:
- schur: bfloat16 [40960, 10240], P(('hyp', 'row'), 'col'), parts along dimension 0
- panel: bfloat16 [40960, 256], P(('hyp', 'row')), parts along dimension 0
The draws below stay inside these ranges and needn't reach their ends.
There are 4 independent parts, one for each index of `hyp`. The reference program is written for one: setup_inputs(seed, part) draws one part's arguments, and reference() takes and returns one part's arrays. A program takes and returns all parts, laid end to end along the dimension named above; each array names one. Nothing has to cross between parts.
Inputs may be any that keep to these rules, and one draw needn't show every extreme that they name: `child_map`: each child's entries are distinct. Parent block p lies on row index p // 5 and column index p // 20. Of the 8 blocks of a child on one row index (child c on row indices c * 8 to (c + 1) * 8 - 1, in order), at most 1 lie on one parent row index; of the 16 blocks on one column index, at most 4 lie on one parent column index. Every parent row index receives the same number of blocks of each child. `child_updates`: each child's update block is symmetric. `front_orig`: Symmetric. `panel_inverse`: upper triangular with a positive diagonal.
All inputs are finite; a program needn't handle non-finite values.
Results may differ from the reference program's by a relative error of at most 0.0052.
Values may be sent and summed in bfloat16 or wider, within the bound.
No kernel may reach another device: no remote copies, remote signals or barrier semaphores. Data moves between devices by JAX's collectives and lax.ppermute only.
A program may use at most 128 MiB of HBM per device.

```python
import math
import jax
import jax.numpy as jnp

F = 10240
C = 8192
B = 128
PANEL = 256
CB = 64
NF = 16
MB = 5
RUN = 8


def draw_front_orig(key, part):
    raw = jax.random.normal(key, (F, F), jnp.float32)
    return ((raw + raw.T) * 0.5).astype(jnp.bfloat16)


def draw_child_updates(key, part):
    raw = jax.random.normal(key, (2, C, C), jnp.float32)
    sym = (raw + jnp.swapaxes(raw, 1, 2)) * 0.5
    return sym.reshape(2 * C, C).astype(jnp.bfloat16)


def draw_child_map(key, part):
    picks = CB // NF
    maps = []
    for child_index in range(2):
        base = jax.random.fold_in(key, 11 + child_index)
        key_owner, key_runs, key_slots = jax.random.split(base, 3)
        owner_perm = jax.random.permutation(key_owner, NF).astype(jnp.int32)
        run_keys = jax.random.split(key_runs, CB // RUN)
        run_perm = jax.vmap(lambda k: jax.random.permutation(k, RUN))(run_keys).astype(jnp.int32)
        order = (jnp.arange(CB // RUN, dtype=jnp.int32)[:, None] * RUN + run_perm).reshape(CB)
        fine = owner_perm[order % NF]
        slot_index = order // NF

        def subset(k):
            key_mid, key_mix = jax.random.split(k)
            middle = (jax.random.permutation(key_mid, MB - 2) + 1).astype(jnp.int32)
            chosen = jnp.concatenate([jnp.array([0, MB - 1], jnp.int32), middle[:picks - 2]])
            return jax.random.permutation(key_mix, chosen).astype(jnp.int32)
        table = jax.vmap(subset)(jax.random.split(key_slots, NF))
        inner = table[fine, slot_index]
        maps.append(fine * MB + inner)
    return jnp.stack(maps).astype(jnp.int32)


def draw_panel_inverse(key, part):
    key_diag, key_off = jax.random.split(key)
    rows_at = jnp.arange(PANEL, dtype=jnp.int32)[:, None]
    cols_at = jnp.arange(PANEL, dtype=jnp.int32)[None, :]
    diag_vals = jnp.exp(jax.random.uniform(key_diag, (PANEL,), jnp.float32, math.log(0.04), math.log(0.15)))
    off_vals = jax.random.normal(key_off, (PANEL, PANEL), jnp.float32) * 0.008
    result = jnp.where(rows_at == cols_at, diag_vals[:, None], jnp.where(cols_at > rows_at, off_vals, 0.0))
    return result.astype(jnp.bfloat16)


def setup_inputs(seed: int = 0, part: int = 0) -> dict:
    seeds = jax.random.split(jax.random.key(seed), 5)
    own_keys = jax.random.split(jax.random.fold_in(seeds[4], part), 5)
    return {
        "front_orig": draw_front_orig(jax.random.fold_in(jax.random.fold_in(seeds[4], part), 71), part),
        "child_updates": draw_child_updates(jax.random.fold_in(jax.random.fold_in(seeds[4], part), 71), part),
        "child_map": draw_child_map(jax.random.fold_in(jax.random.fold_in(seeds[4], part), 71), part),
        "panel_inverse": draw_panel_inverse(jax.random.fold_in(jax.random.fold_in(seeds[4], part), 71), part),
    }


def reference(front_orig, child_updates, child_map, panel_inverse):
    offsets = jnp.arange(B, dtype=jnp.int32)
    front32 = front_orig.astype(jnp.float32)
    for child_index in range(2):
        update_block = child_updates[child_index * C:(child_index + 1) * C].astype(jnp.float32)
        indices = (child_map[child_index].astype(jnp.int32)[:, None] * B + offsets[None, :]).reshape(C).astype(jnp.int32)
        front32 = front32.at[indices[:, None], indices[None, :]].add(update_block)
    front = front32.astype(jnp.bfloat16)
    panel = jnp.dot(front[:, :PANEL], panel_inverse, preferred_element_type=jnp.float32).astype(jnp.bfloat16)
    update = jnp.dot(panel, panel.T, preferred_element_type=jnp.float32)
    schur = (front.astype(jnp.float32) - update).astype(jnp.bfloat16)
    return schur, panel
```

```python
import jax
import jax.numpy as jnp
from jax import lax
from jax.experimental import pallas as pl
from jax.experimental.pallas import tpu as pltpu
from jax.sharding import PartitionSpec as P


SMEM = pltpu.MemorySpace.SMEM
VMEM = pltpu.MemorySpace.VMEM
NR = 16
NC = 4
CB = 64
MB = 5
QB = 20
FB = 80


def tables_kernel(map_ref, pos_ref, jl_ref, sel_ref, krow_ref, kcol_ref, inv_ref, cnt_ref):
    row = pos_ref[0]
    col = pos_ref[1]
    child = row // 8
    group = (row % 8) // 2

    def clear(i, _):
        inv_ref[i] = -1
        return 0

    lax.fori_loop(0, 2 * FB, clear, 0, unroll=8)

    def invert(i, _):
        inv_ref[(i // CB) * FB + map_ref[i]] = i % CB
        return 0

    lax.fori_loop(0, 2 * CB, invert, 0, unroll=8)

    def rows(r, _):
        count = 0
        for p in range(MB):
            v = inv_ref[child * FB + r * MB + p]
            hit = v >= 0
            jl_ref[jnp.where(hit, r * 4 + count, CB)] = v
            count = count + hit.astype(jnp.int32)
        return 0

    lax.fori_loop(0, NR, rows, 0)
    for c in range(2):
        count = 0
        for p in range(MB):
            hit = inv_ref[c * FB + row * MB + p] >= 0
            krow_ref[c * MB + p] = jnp.where(hit, count, -1)
            count = count + hit.astype(jnp.int32)
        for g in range(5):
            cnt_ref[g] = 0

        def column(q, _):
            v = inv_ref[c * FB + col * QB + q]
            hit = v >= 0
            g = jnp.where(hit, v // 16, 4)
            rank = cnt_ref[g]
            cnt_ref[g] = rank + 1
            kcol_ref[c * QB + q] = jnp.where(hit, (g * 2 + rank % 2) * 2 + rank // 2, -1)
            return 0

        lax.fori_loop(0, QB, column, 0)
    for y in range(NC):

        def pick(q, count):
            v = inv_ref[child * FB + y * QB + q]
            hit = jnp.logical_and(v >= 0, v // 16 == group)
            sel_ref[jnp.where(hit, y * 4 + count, 16)] = v % 16
            return count + hit.astype(jnp.int32)

        lax.fori_loop(0, QB, pick, jnp.int32(0))


def tables(flat_map, pos):
    shapes = [CB + 16, 32, 16, 48]
    return pl.pallas_call(
        tables_kernel,
        out_shape=[jax.ShapeDtypeStruct((n,), jnp.int32) for n in shapes],
        in_specs=[pl.BlockSpec(memory_space=SMEM)] * 2,
        out_specs=[pl.BlockSpec(memory_space=SMEM)] * 4,
        scratch_shapes=[pltpu.SMEM((2 * FB,), jnp.int32), pltpu.SMEM((8,), jnp.int32)],
        name="tables",
    )(flat_map, pos)


def pack_columns(sel, pos, own, other, chunk):
    block = own.shape[0] // 8

    def kernel(sel_ref, pos_ref, own_ref, other_ref, out_ref, sem):
        core = pos_ref[0] % 2
        for y in range(NC):
            index = sel_ref[y * 4 + 2 * chunk + core]
            start = pl.multiple_of((index % 8) * block, block)
            mine = index // 8 == core

            @pl.when(mine)
            def _():
                pltpu.make_async_copy(own_ref.at[pl.ds(start, block)], out_ref.at[y], sem.at[y]).start()

            @pl.when(jnp.logical_not(mine))
            def _():
                pltpu.make_async_copy(other_ref.at[pl.ds(start, block)], out_ref.at[y], sem.at[y]).start()

        for y in range(NC):
            pltpu.make_async_copy(own_ref.at[pl.ds(0, block)], out_ref.at[y], sem.at[y]).wait()

    return pl.pallas_call(
        kernel,
        out_shape=jax.ShapeDtypeStruct((NC, block, own.shape[1]), own.dtype),
        in_specs=[pl.BlockSpec(memory_space=SMEM)] * 2 + [pl.BlockSpec(memory_space=pl.ANY)] * 2,
        out_specs=pl.BlockSpec(memory_space=pl.ANY),
        scratch_shapes=[pltpu.SemaphoreType.DMA((NC,))],
        name=f"pack_columns_{chunk}",
    )(sel, pos, own, other)


def pack_rows(jl, columns, chunk):
    block = columns.shape[1]

    def kernel(jl_ref, in_ref, out_ref):
        def one(r, _):
            for k in range(4):
                j = jl_ref[r * 4 + k]
                start = pl.multiple_of((j % 16) * block, block)
                out_ref[r, :, k * block : (k + 1) * block] = in_ref[j // 16, :, pl.ds(start, block)]
            return 0

        lax.fori_loop(0, NR, one, 0)

    return pl.pallas_call(
        kernel,
        out_shape=jax.ShapeDtypeStruct((NR, block, 4 * block), columns.dtype),
        in_specs=[pl.BlockSpec(memory_space=SMEM), pl.BlockSpec(memory_space=VMEM)],
        out_specs=pl.BlockSpec(memory_space=VMEM),
        name=f"pack_rows_{chunk}",
    )(jl, columns)


def fill_eyes(eye_ref):
    block = eye_ref.shape[1]
    i = lax.broadcasted_iota(jnp.int32, (block, block), 0)
    j = lax.broadcasted_iota(jnp.int32, (block, block), 1)
    eye = (i == j).astype(jnp.float32).astype(jnp.bfloat16)
    zero = jnp.zeros((block, block), jnp.bfloat16)
    for v in range(4):
        eye_ref[v, :, :block] = eye if v & 1 else zero
        eye_ref[v, :, block:] = eye if v & 2 else zero


def front_tile(orig, read, krow_ref, kcol_ref, eye_ref, p, q):
    parts = []
    bits = 0
    for c in range(2):
        k = krow_ref[c * MB + p]
        e = kcol_ref[c * QB + q]
        bits = bits + jnp.where(jnp.logical_and(k >= 0, e >= 0), 1 << c, 0)
        parts.append(read(c, jnp.maximum(k, 0), jnp.maximum(e, 0)))
    both = jnp.concatenate(parts, axis=1)
    added = lax.dot_general(
        eye_ref[bits], both, (((1,), (1,)), ((), ())), preferred_element_type=jnp.float32
    )
    return (orig.astype(jnp.float32) + added).astype(jnp.bfloat16)


def strip_panel(krow, kcol, arrived, front_orig, panel_inverse):
    block = arrived.shape[1]
    rows = front_orig.shape[0]

    def kernel(krow_ref, kcol_ref, arrived_ref, orig_ref, inverse_ref, out_ref, eye_ref):
        fill_eyes(eye_ref)

        def read(c, k, e):
            start = pl.multiple_of(k * block, block)
            return arrived_ref[c * 8 + e // 2, :, pl.ds(start, block)]

        for p in range(MB):
            here = slice(p * block, (p + 1) * block)
            tiles = [
                front_tile(
                    orig_ref[here, q * block : (q + 1) * block],
                    read, krow_ref, kcol_ref, eye_ref, p, q,
                )
                for q in range(2)
            ]
            out_ref[here, :] = jnp.dot(
                jnp.concatenate(tiles, axis=1), inverse_ref[...], preferred_element_type=jnp.float32
            ).astype(jnp.bfloat16)

    return pl.pallas_call(
        kernel,
        grid=(1,),
        out_shape=jax.ShapeDtypeStruct((rows, 2 * block), jnp.bfloat16),
        in_specs=[
            pl.BlockSpec(memory_space=SMEM),
            pl.BlockSpec(memory_space=SMEM),
            pl.BlockSpec(memory_space=VMEM),
            pl.BlockSpec((rows, 2 * block), lambda i: (0, 0)),
            pl.BlockSpec(memory_space=VMEM),
        ],
        out_specs=pl.BlockSpec(memory_space=VMEM),
        scratch_shapes=[pltpu.VMEM((4, block, 2 * block), jnp.bfloat16)],
        name="strip_panel",
    )(krow, kcol, arrived, front_orig, panel_inverse)


def assemble(krow, kcol, first, second, front_orig):
    block = first.shape[1]

    def kernel(krow_ref, kcol_ref, first_ref, second_ref, orig_ref, out_ref, buf_ref, eye_ref, sem):
        copies = [
            pltpu.make_async_copy(ref, buf_ref.at[t], sem.at[t])
            for t, ref in enumerate((first_ref, second_ref))
        ]
        for copy in copies:
            copy.start()
        fill_eyes(eye_ref)
        for copy in copies:
            copy.wait()

        def read(c, k, e):
            start = pl.multiple_of(k * block, block)
            return buf_ref[e % 2, c * 8 + e // 2, :, pl.ds(start, block)]

        def column(q, _):
            cols = pl.ds(pl.multiple_of(q * block, block), block)
            for p in range(MB):
                here = slice(p * block, (p + 1) * block)
                out_ref[here, cols] = front_tile(
                    orig_ref[here, cols], read, krow_ref, kcol_ref, eye_ref, p, q
                )
            return 0

        lax.fori_loop(0, QB, column, 0)

    return pl.pallas_call(
        kernel,
        out_shape=jax.ShapeDtypeStruct(front_orig.shape, jnp.bfloat16),
        in_specs=[pl.BlockSpec(memory_space=SMEM)] * 2
        + [pl.BlockSpec(memory_space=pl.ANY)] * 2
        + [pl.BlockSpec(memory_space=VMEM)],
        out_specs=pl.BlockSpec(memory_space=VMEM),
        scratch_shapes=[
            pltpu.VMEM((2,) + first.shape, jnp.bfloat16),
            pltpu.VMEM((4, block, 2 * block), jnp.bfloat16),
            pltpu.SemaphoreType.DMA((2,)),
        ],
        name="assemble",
    )(krow, kcol, first, second, front_orig)


def device(x, z, core, y):
    return ((x * 2 + z) * 2 + core) * NC + y


def moved(array, pairs):
    return lax.ppermute(array, ("row", "col"), pairs)


PLACES = [(x, z, core) for x in range(4) for z in range(2) for core in range(2)]


def local(front_orig, child_updates, child_map, panel_inverse):
    me_row = lax.axis_index("row")
    me_col = lax.axis_index("col")
    me_x = me_row // 4
    me_z = (me_row // 2) % 2
    me_core = me_row % 2
    pos = jnp.stack([me_row, me_col]).astype(jnp.int32)
    other = lax.ppermute(child_updates, "row", [(r, r ^ 1) for r in range(NR)])
    jl, sel, krow, kcol = tables(child_map.reshape(-1), pos)

    sent = pack_columns(sel, pos, child_updates, other, 0)
    columns = lax.all_to_all(sent, "col", 0, 0, tiled=True)
    first = lax.all_to_all(pack_rows(jl, columns, 0), "row", 0, 0, tiled=True)

    panel_0 = strip_panel(krow, kcol, first, front_orig, panel_inverse)
    child_b, other_b, panel_0 = lax.optimization_barrier((child_updates, other, panel_0))
    sent = pack_columns(sel, pos, child_b, other_b, 1)
    columns = lax.all_to_all(sent, "col", 0, 0, tiled=True)
    across_z = moved(panel_0, [(device(x, z, k, 0), device(x, 1 - z, k, 0)) for x, z, k in PLACES])

    spread = [
        moved(panel_0, [(device(x, z, k, 0), device(x, z, k, y)) for x, z, k in PLACES])
        for y in range(1, NC)
    ]
    turned = moved(
        across_z, [(device(x, z, k, 0), device(x, z, k, x)) for x, z, k in PLACES if x > 0]
    )
    second = lax.all_to_all(pack_rows(jl, columns, 1), "row", 0, 0, tiled=True)

    row_panel = jnp.where(me_col == 0, panel_0, spread[0] + spread[1] + spread[2])
    facing = jnp.where(me_col == 0, across_z, turned)
    pair = jnp.stack([row_panel, facing])
    sides = [
        moved(pair, [(device(x, z, k, x), device((x + d) % 4, z, k, x)) for x, z, k in PLACES])
        for d in range(1, 4)
    ]
    pair = jnp.where(me_x == me_col, pair, sides[0] + sides[1] + sides[2])
    pair = jnp.where(me_z == 0, pair, pair[::-1])
    swapped = lax.ppermute(pair, "row", [(r, r ^ 1) for r in range(NR)])
    col_panel = jnp.stack(
        [jnp.where(me_core == 0, pair, swapped), jnp.where(me_core == 0, swapped, pair)], axis=1
    ).reshape(-1, pair.shape[-1])

    front = assemble(krow, kcol, first, second, front_orig)
    update = lax.dot_general(
        row_panel, col_panel, (((1,), (1,)), ((), ())), preferred_element_type=jnp.float32
    )
    schur = (front.astype(jnp.float32) - update).astype(jnp.bfloat16)
    return (schur, row_panel)


def solution(mesh):
    in_specs = (P(("hyp", "row"), "col"), P(("hyp", "row"), "col"), P("hyp", None), P("hyp", None))
    out_specs = (P(("hyp", "row"), "col"), P(("hyp", "row"), None))
    return jax.shard_map(local, mesh=mesh, in_specs=in_specs, out_specs=out_specs, check_vma=False)
```

```python
import jax
import jax.numpy as jnp
from jax import lax
from jax.experimental import pallas as pl
from jax.experimental.pallas import tpu as pltpu
from jax.sharding import Mesh, PartitionSpec as P


SMEM = pltpu.MemorySpace.SMEM
VMEM = pltpu.MemorySpace.VMEM
CB = 64
MB = 5
QB = 20
FB = 80
PLACES = [(x, z, core) for x in range(4) for z in range(2) for core in range(2)]


def params(mib):
    return pltpu.CompilerParams(vmem_limit_bytes=mib << 20)


def tables_kernel(map_ref, pos_ref, sel_ref, jsel_ref, jl_ref, krow_ref, kcol_ref, inv_ref, cnt_ref):
    row = pos_ref[0]
    col = pos_ref[1]
    x = row // 4
    zk = row % 4
    child = row // 8
    group = (row % 8) // 2

    def clear(i, _):
        inv_ref[i] = -1
        return 0

    lax.fori_loop(0, 2 * FB, clear, 0, unroll=8)
    for c in range(2):

        def invert(i, _):
            inv_ref[c * FB + map_ref[c, i]] = i
            return 0

        lax.fori_loop(0, CB, invert, 0, unroll=8)
    for y in range(4):

        def pick(q, counts):
            v = inv_ref[child * FB + y * QB + q]
            hit = jnp.logical_and(v >= 0, v // 16 == group)
            sel_ref[jnp.where(hit, y * 4 + counts[0], 16)] = v % 16
            hit_j = jnp.logical_and(v >= 0, v // 16 == col)
            jsel_ref[jnp.where(hit_j, y * 4 + counts[1], 16)] = v % 16
            return counts[0] + hit.astype(jnp.int32), counts[1] + hit_j.astype(jnp.int32)

        lax.fori_loop(0, QB, pick, (jnp.int32(0), jnp.int32(0)))
    for c in range(2):
        count = 0
        for p in range(MB):
            hit = inv_ref[c * FB + row * MB + p] >= 0
            krow_ref[c * MB + p] = jnp.where(hit, count, -1)
            count = count + hit.astype(jnp.int32)
        for g in range(10):
            cnt_ref[g] = 0

        def arrive(q, _):
            v = inv_ref[c * FB + col * QB + q]
            hit = v >= 0
            g = jnp.where(hit, v // 16, 4)
            rank = cnt_ref[g]
            cnt_ref[g] = rank + 1
            sender = ((g % 2) * 2 + rank % 2) ^ zk
            kcol_ref[c * QB + q] = jnp.where(hit, ((rank // 2) * 4 + sender) * 4 + c * 2 + g // 2, -1)
            return 0

        lax.fori_loop(0, QB, arrive, 0)
        for d in range(4):

            def pass_on(q, count):
                v = inv_ref[c * FB + x * QB + d * MB + q]
                hit = v >= 0
                g = jnp.where(hit, v // 16, 4)
                slot = cnt_ref[5 + g]
                cnt_ref[5 + g] = slot + 1
                jl_ref[jnp.where(hit, c * 16 + d * 4 + count, 32)] = g * 4 + slot
                return count + hit.astype(jnp.int32)

            lax.fori_loop(0, MB, pass_on, jnp.int32(0))


def tables(child_map, pos):
    shapes = [32, 32, 48, 16, 48]
    return pl.pallas_call(
        tables_kernel,
        out_shape=[jax.ShapeDtypeStruct((n,), jnp.int32) for n in shapes],
        in_specs=[pl.BlockSpec(memory_space=SMEM)] * 2,
        out_specs=[pl.BlockSpec(memory_space=SMEM)] * 5,
        scratch_shapes=[pltpu.SMEM((2 * FB,), jnp.int32), pltpu.SMEM((16,), jnp.int32)],
        compiler_params=params(4),
        name="tables",
    )(child_map, pos)


def pack_first(sel, jsel, pos, own, other, chunk):
    block = own.shape[0] // 8

    def kernel(sel_ref, jsel_ref, pos_ref, own_ref, other_ref, out_ref, sem):
        core = pos_ref[0] % 2
        for y in range(4):
            index = sel_ref[y * 4 + 2 * chunk + core]
            rows = pl.ds(pl.multiple_of((index % 8) * block, block), block)
            mine = index // 8 == core

            def copy(ref):
                for x in range(4):
                    for k in range(4):
                        cols = pl.ds(pl.multiple_of(jsel_ref[x * 4 + k] * block, block), block)
                        pltpu.make_async_copy(
                            ref.at[rows, cols],
                            out_ref.at[x * 4 + y, :, pl.ds(k * block, block)],
                            sem,
                        ).start()

            pl.when(mine)(lambda: copy(own_ref))
            pl.when(jnp.logical_not(mine))(lambda: copy(other_ref))

        pltpu.make_async_copy(out_ref, out_ref, sem).wait()

    return pl.pallas_call(
        kernel,
        out_shape=jax.ShapeDtypeStruct((16, block, 4 * block), own.dtype),
        in_specs=[pl.BlockSpec(memory_space=SMEM)] * 3 + [pl.BlockSpec(memory_space=pltpu.MemorySpace.HBM)] * 2,
        out_specs=pl.BlockSpec(memory_space=VMEM),
        scratch_shapes=[pltpu.SemaphoreType.DMA(())],
        compiler_params=params(8),
    )(sel, jsel, pos, own, other)


def pack_second(jl, pos, arrived):
    block = arrived.shape[1]

    def kernel(jl_ref, pos_ref, in_ref, *out_refs):
        zk = pos_ref[0] % 4
        for d in range(4):
            for xs in range(4):
                for k in range(4):
                    code = jl_ref[(xs // 2) * 16 + (zk ^ d) * 4 + k]
                    cols = pl.ds(pl.multiple_of((code % 4) * block, block), block)
                    out_refs[d][xs, :, k * block : (k + 1) * block] = in_ref[
                        xs * 4 + code // 4, :, cols
                    ]

    return pl.pallas_call(
        kernel,
        out_shape=[jax.ShapeDtypeStruct((4, block, 4 * block), arrived.dtype)] * 4,
        in_specs=[pl.BlockSpec(memory_space=SMEM)] * 2 + [pl.BlockSpec(memory_space=VMEM)],
        out_specs=[pl.BlockSpec(memory_space=VMEM)] * 4,
        compiler_params=params(8),
    )(jl, pos, arrived)


def fill_eyes(eye_ref):
    block = eye_ref.shape[1]
    i = lax.broadcasted_iota(jnp.int32, (block, block), 0)
    j = lax.broadcasted_iota(jnp.int32, (block, block), 1)
    eye = (i == j).astype(jnp.float32).astype(jnp.bfloat16)
    zero = jnp.zeros((block, block), jnp.bfloat16)
    for v in range(4):
        eye_ref[v, :, :block] = eye if v & 1 else zero
        eye_ref[v, :, block:] = eye if v & 2 else zero


def front_tile(orig, buf_ref, krow_ref, kcol_ref, eye_ref, p, q):
    block = orig.shape[0]
    parts = []
    bits = 0
    for c in range(2):
        k = krow_ref[c * MB + p]
        e = kcol_ref[c * QB + q]
        bits = bits + jnp.where(jnp.logical_and(k >= 0, e >= 0), 1 << c, 0)
        start = pl.multiple_of(jnp.maximum(k, 0) * block, block)
        parts.append(buf_ref[jnp.maximum(e, 0), :, pl.ds(start, block)])
    both = jnp.concatenate(parts, axis=1)
    added = lax.dot_general(
        eye_ref[bits], both, (((1,), (1,)), ((), ())), preferred_element_type=jnp.float32
    )
    return (orig.astype(jnp.float32) + added).astype(jnp.bfloat16)


def gather(refs, buf_ref, sem, meanwhile):
    copies = [
        pltpu.make_async_copy(ref, buf_ref.at[pl.ds(4 * n, 4)], sem.at[n])
        for n, ref in enumerate(refs)
    ]
    for copy in copies:
        copy.start()
    meanwhile()
    for copy in copies:
        copy.wait()


def strip_panel(krow, kcol, arrived, front_orig, panel_inverse):
    block = arrived[0].shape[1]
    rows = front_orig.shape[0]

    def kernel(krow_ref, kcol_ref, a0, a1, a2, a3, orig_ref, inverse_ref, out_ref, buf_ref, eye_ref, sem):
        gather((a0, a1, a2, a3), buf_ref, sem, lambda: fill_eyes(eye_ref))
        for p in range(MB):
            here = slice(p * block, (p + 1) * block)
            tiles = [
                front_tile(
                    orig_ref[here, q * block : (q + 1) * block],
                    buf_ref, krow_ref, kcol_ref, eye_ref, p, q,
                )
                for q in range(2)
            ]
            out_ref[here, :] = jnp.dot(
                jnp.concatenate(tiles, axis=1), inverse_ref[...], preferred_element_type=jnp.float32
            ).astype(jnp.bfloat16)

    return pl.pallas_call(
        kernel,
        grid=(1,),
        out_shape=jax.ShapeDtypeStruct((rows, 2 * block), jnp.bfloat16),
        in_specs=[pl.BlockSpec(memory_space=SMEM)] * 2
        + [pl.BlockSpec(memory_space=pl.ANY)] * 4
        + [
            pl.BlockSpec((rows, 2 * block), lambda i: (0, 0)),
            pl.BlockSpec(memory_space=VMEM),
        ],
        out_specs=pl.BlockSpec(memory_space=VMEM),
        scratch_shapes=[
            pltpu.VMEM((16, block, 4 * block), jnp.bfloat16),
            pltpu.VMEM((4, block, 2 * block), jnp.bfloat16),
            pltpu.SemaphoreType.DMA((4,)),
        ],
        compiler_params=params(12),
        name="strip_panel",
    )(krow, kcol, *arrived, front_orig, panel_inverse)


def assemble(krow, kcol, arrived, front_orig):
    block = arrived[0].shape[1]

    def kernel(krow_ref, kcol_ref, *refs):
        orig_ref, out_ref, buf_ref, eye_ref, sem = refs[8:]
        gather(refs[:8], buf_ref, sem, lambda: fill_eyes(eye_ref))

        def column(q, _):
            cols = pl.ds(pl.multiple_of(q * block, block), block)
            for p in range(MB):
                here = slice(p * block, (p + 1) * block)
                out_ref[here, cols] = front_tile(
                    orig_ref[here, cols], buf_ref, krow_ref, kcol_ref, eye_ref, p, q
                )
            return 0

        lax.fori_loop(0, QB, column, 0)

    return pl.pallas_call(
        kernel,
        out_shape=jax.ShapeDtypeStruct(front_orig.shape, jnp.bfloat16),
        in_specs=[pl.BlockSpec(memory_space=SMEM)] * 2
        + [pl.BlockSpec(memory_space=pl.ANY)] * 8
        + [pl.BlockSpec(memory_space=VMEM)],
        out_specs=pl.BlockSpec(memory_space=VMEM),
        scratch_shapes=[
            pltpu.VMEM((32, block, 4 * block), jnp.bfloat16),
            pltpu.VMEM((4, block, 2 * block), jnp.bfloat16),
            pltpu.SemaphoreType.DMA((8,)),
        ],
        compiler_params=params(24),
        name="assemble",
    )(krow, kcol, *arrived, front_orig)


def device(x, z, core, y):
    return ((x * 2 + z) * 2 + core) * 4 + y


def moved(array, pairs):
    return lax.ppermute(array, ("x", "z", "core", "col"), pairs)


def over_zk(array, d):
    return lax.ppermute(array, ("z", "core"), [(r, r ^ d) for r in range(4)])


def local(front_orig, child_updates, child_map, panel_inverse):
    me_x = lax.axis_index("x")
    me_z = lax.axis_index("z")
    me_core = lax.axis_index("core")
    me_col = lax.axis_index("col")
    pos = jnp.stack([me_x * 4 + me_z * 2 + me_core, me_col]).astype(jnp.int32)
    other = over_zk(child_updates, 1)
    sel, jsel, jl, krow, kcol = tables(child_map, pos)

    outs = []
    for chunk in range(2):
        sent = pack_first(sel, jsel, pos, child_updates, other, chunk)
        part = lax.all_to_all(sent, ("x", "col"), 0, 0, tiled=True)
        outs.append(pack_second(jl, pos, part))
    first = [outs[0][0]] + [over_zk(outs[0][d], d) for d in (1, 2, 3)]
    first, outs[1] = lax.optimization_barrier((first, outs[1]))
    second = [outs[1][0]] + [over_zk(outs[1][d], d) for d in (1, 2, 3)]

    panel_0 = strip_panel(krow, kcol, first, front_orig, panel_inverse)
    spread = [
        moved(panel_0, [(device(x, z, k, 0), device(x, z, k, y)) for x, z, k in PLACES])
        for y in range(1, 4)
    ]
    row_panel = jnp.where(me_col == 0, panel_0, spread[0] + spread[1] + spread[2])
    sides = [
        moved(row_panel, [(device(x, z, k, x), device((x + d) % 4, z, k, x)) for x, z, k in PLACES])
        for d in range(1, 4)
    ]
    piece = jnp.where(me_x == me_col, row_panel, sides[0] + sides[1] + sides[2])
    across = over_zk(piece, 2)
    pair = jnp.stack([jnp.where(me_z == 0, piece, across), jnp.where(me_z == 0, across, piece)])
    swapped = over_zk(pair, 1)
    col_panel = jnp.stack(
        [jnp.where(me_core == 0, pair, swapped), jnp.where(me_core == 0, swapped, pair)], axis=1
    ).reshape(-1, pair.shape[-1])

    front = assemble(krow, kcol, first + second, front_orig)
    update = lax.dot_general(
        row_panel, col_panel, (((1,), (1,)), ((), ())), preferred_element_type=jnp.float32
    )
    schur = (front.astype(jnp.float32) - update).astype(jnp.bfloat16)
    return (schur, row_panel)


def solution(mesh):
    rows = ("hyp", "x", "z", "core")
    split = Mesh(mesh.devices.reshape(-1, 4, 2, 2, 4), rows + ("col",))
    in_specs = (P(rows, "col"), P(rows, "col"), P("hyp", None), P("hyp", None))
    out_specs = (P(rows, "col"), P(rows, None))
    return jax.shard_map(local, mesh=split, in_specs=in_specs, out_specs=out_specs, check_vma=False)
```

```python
import jax
import jax.numpy as jnp
from jax import lax
from jax.experimental import pallas as pl
from jax.experimental.pallas import tpu as pltpu
from jax.sharding import Mesh, PartitionSpec as P


SMEM = pltpu.MemorySpace.SMEM
VMEM = pltpu.MemorySpace.VMEM
CB = 64
MB = 5
QB = 20
FB = 80
PLACES = [(x, z, core) for x in range(4) for z in range(2) for core in range(2)]


def params(mib):
    return pltpu.CompilerParams(vmem_limit_bytes=mib << 20)


def tables_kernel(map_ref, pos_ref, sel_ref, jsel_ref, jl_ref, krow_ref, kcol_ref, inv_ref, cnt_ref):
    row = pos_ref[0]
    col = pos_ref[1]
    x = row // 4
    zk = row % 4
    child = row // 8
    group = (row % 8) // 2

    def clear(i, _):
        inv_ref[i] = -1
        return 0

    lax.fori_loop(0, 2 * FB, clear, 0, unroll=8)
    for c in range(2):

        def invert(i, _):
            inv_ref[c * FB + map_ref[c, i]] = i
            return 0

        lax.fori_loop(0, CB, invert, 0, unroll=8)
    for y in range(4):

        def pick(q, counts):
            v = inv_ref[child * FB + y * QB + q]
            hit = jnp.logical_and(v >= 0, v // 16 == group)
            sel_ref[jnp.where(hit, y * 4 + counts[0], 16)] = v % 16
            hit_j = jnp.logical_and(v >= 0, v // 16 == col)
            jsel_ref[jnp.where(hit_j, y * 4 + counts[1], 16)] = v % 16
            return counts[0] + hit.astype(jnp.int32), counts[1] + hit_j.astype(jnp.int32)

        lax.fori_loop(0, QB, pick, (jnp.int32(0), jnp.int32(0)))
    for c in range(2):
        count = 0
        for p in range(MB):
            hit = inv_ref[c * FB + row * MB + p] >= 0
            krow_ref[c * MB + p] = jnp.where(hit, count, -1)
            count = count + hit.astype(jnp.int32)
        for g in range(10):
            cnt_ref[g] = 0

        def arrive(q, _):
            v = inv_ref[c * FB + col * QB + q]
            hit = v >= 0
            g = jnp.where(hit, v // 16, 4)
            rank = cnt_ref[g]
            cnt_ref[g] = rank + 1
            sender = ((g % 2) * 2 + rank % 2) ^ zk
            kcol_ref[c * QB + q] = jnp.where(hit, ((rank // 2) * 4 + sender) * 4 + c * 2 + g // 2, -1)
            return 0

        lax.fori_loop(0, QB, arrive, 0)
        for d in range(4):

            def pass_on(q, count):
                v = inv_ref[c * FB + x * QB + d * MB + q]
                hit = v >= 0
                g = jnp.where(hit, v // 16, 4)
                slot = cnt_ref[5 + g]
                cnt_ref[5 + g] = slot + 1
                jl_ref[jnp.where(hit, c * 16 + d * 4 + count, 32)] = g * 4 + slot
                return count + hit.astype(jnp.int32)

            lax.fori_loop(0, MB, pass_on, jnp.int32(0))


def tables(child_map, pos):
    shapes = [32, 32, 48, 16, 48]
    return pl.pallas_call(
        tables_kernel,
        out_shape=[jax.ShapeDtypeStruct((n,), jnp.int32) for n in shapes],
        in_specs=[pl.BlockSpec(memory_space=SMEM)] * 2,
        out_specs=[pl.BlockSpec(memory_space=SMEM)] * 5,
        scratch_shapes=[pltpu.SMEM((2 * FB,), jnp.int32), pltpu.SMEM((16,), jnp.int32)],
        compiler_params=params(63),
        name="tables",
    )(child_map, pos)


def pack_first(sel, jsel, pos, own, other, chunk):
    block = own.shape[0] // 8
    half = block // 2

    def kernel(sel_ref, jsel_ref, pos_ref, own_ref, other_ref, out_ref, sem):
        core = pos_ref[0] % 2
        for y in range(4):
            index = sel_ref[y * 4 + 2 * (chunk // 2) + core]
            rows = pl.ds(pl.multiple_of((index % 8) * block + (chunk % 2) * half, half), half)
            mine = index // 8 == core

            def copy(ref):
                for x in range(4):
                    for k in range(4):
                        cols = pl.ds(pl.multiple_of(jsel_ref[x * 4 + k] * block, block), block)
                        pltpu.make_async_copy(
                            ref.at[rows, cols],
                            out_ref.at[x * 4 + y, :, pl.ds(k * block, block)],
                            sem,
                        ).start()

            pl.when(mine)(lambda: copy(own_ref))
            pl.when(jnp.logical_not(mine))(lambda: copy(other_ref))

        pltpu.make_async_copy(out_ref, out_ref, sem).wait()

    return pl.pallas_call(
        kernel,
        out_shape=jax.ShapeDtypeStruct((16, half, 4 * block), own.dtype),
        in_specs=[pl.BlockSpec(memory_space=SMEM)] * 3 + [pl.BlockSpec(memory_space=pltpu.MemorySpace.HBM)] * 2,
        out_specs=pl.BlockSpec(memory_space=VMEM),
        scratch_shapes=[pltpu.SemaphoreType.DMA(())],
        compiler_params=params(63),
    )(sel, jsel, pos, own, other)


def pack_second(jl, pos, arrived):
    block = arrived.shape[2] // 4

    def kernel(jl_ref, pos_ref, in_ref, *out_refs):
        zk = pos_ref[0] % 4
        for d in range(4):
            for xs in range(4):
                for k in range(4):
                    code = jl_ref[(xs // 2) * 16 + (zk ^ d) * 4 + k]
                    cols = pl.ds(pl.multiple_of((code % 4) * block, block), block)
                    out_refs[d][xs, :, k * block : (k + 1) * block] = in_ref[
                        xs * 4 + code // 4, :, cols
                    ]

    return pl.pallas_call(
        kernel,
        out_shape=[jax.ShapeDtypeStruct((4,) + arrived.shape[1:], arrived.dtype)] * 4,
        in_specs=[pl.BlockSpec(memory_space=SMEM)] * 2 + [pl.BlockSpec(memory_space=VMEM)],
        out_specs=[pl.BlockSpec(memory_space=VMEM)] * 4,
        compiler_params=params(63),
    )(jl, pos, arrived)


def fill_eyes(eye_ref):
    block = eye_ref.shape[1]
    i = lax.broadcasted_iota(jnp.int32, (block, block), 0)
    j = lax.broadcasted_iota(jnp.int32, (block, block), 1)
    eye = (i == j).astype(jnp.float32).astype(jnp.bfloat16)
    zero = jnp.zeros((block, block), jnp.bfloat16)
    for v in range(4):
        eye_ref[v, :, :block] = eye if v & 1 else zero
        eye_ref[v, :, block:] = eye if v & 2 else zero


def front_tile(orig, buf_ref, krow_ref, kcol_ref, eye_ref, p, q):
    block = orig.shape[0]
    parts = []
    bits = 0
    for c in range(2):
        k = krow_ref[c * MB + p]
        e = kcol_ref[c * QB + q]
        bits = bits + jnp.where(jnp.logical_and(k >= 0, e >= 0), 1 << c, 0)
        start = pl.multiple_of(jnp.maximum(k, 0) * block, block)
        parts.append(buf_ref[jnp.maximum(e, 0), :, pl.ds(start, block)])
    both = jnp.concatenate(parts, axis=1)
    added = lax.dot_general(
        eye_ref[bits], both, (((1,), (1,)), ((), ())), preferred_element_type=jnp.float32
    )
    return (orig.astype(jnp.float32) + added).astype(jnp.bfloat16)


def gather(refs, buf_ref, sem, meanwhile):
    half = buf_ref.shape[1] // 2
    copies = [
        pltpu.make_async_copy(
            ref,
            buf_ref.at[pl.ds((n // 8) * 16 + (n % 4) * 4, 4), pl.ds((n // 4 % 2) * half, half)],
            sem.at[n],
        )
        for n, ref in enumerate(refs)
    ]
    for copy in copies:
        copy.start()
    meanwhile()
    for copy in copies:
        copy.wait()


def strip_panel(krow, kcol, arrived, front_orig, panel_inverse):
    block = arrived[0].shape[2] // 4
    rows = front_orig.shape[0]

    def kernel(krow_ref, kcol_ref, *refs):
        orig_ref, inverse_ref, out_ref, buf_ref, eye_ref, sem = refs[8:]
        gather(refs[:8], buf_ref, sem, lambda: fill_eyes(eye_ref))
        for p in range(MB):
            here = slice(p * block, (p + 1) * block)
            tiles = [
                front_tile(
                    orig_ref[here, q * block : (q + 1) * block],
                    buf_ref, krow_ref, kcol_ref, eye_ref, p, q,
                )
                for q in range(2)
            ]
            out_ref[here, :] = jnp.dot(
                jnp.concatenate(tiles, axis=1), inverse_ref[...], preferred_element_type=jnp.float32
            ).astype(jnp.bfloat16)

    return pl.pallas_call(
        kernel,
        grid=(1,),
        out_shape=jax.ShapeDtypeStruct((rows, 2 * block), jnp.bfloat16),
        in_specs=[pl.BlockSpec(memory_space=SMEM)] * 2
        + [pl.BlockSpec(memory_space=pl.ANY)] * 8
        + [
            pl.BlockSpec((rows, 2 * block), lambda i: (0, 0)),
            pl.BlockSpec(memory_space=VMEM),
        ],
        out_specs=pl.BlockSpec(memory_space=VMEM),
        scratch_shapes=[
            pltpu.VMEM((16, block, 4 * block), jnp.bfloat16),
            pltpu.VMEM((4, block, 2 * block), jnp.bfloat16),
            pltpu.SemaphoreType.DMA((8,)),
        ],
        compiler_params=params(63),
        name="strip_panel",
    )(krow, kcol, *arrived, front_orig, panel_inverse)


def assemble(krow, kcol, arrived, front_orig):
    block = arrived[0].shape[2] // 4

    def kernel(krow_ref, kcol_ref, *refs):
        orig_ref, out_ref, buf_ref, eye_ref, sem = refs[16:]
        gather(refs[:16], buf_ref, sem, lambda: fill_eyes(eye_ref))

        def column(q, _):
            cols = pl.ds(pl.multiple_of(q * block, block), block)
            for p in range(MB):
                here = slice(p * block, (p + 1) * block)
                out_ref[here, cols] = front_tile(
                    orig_ref[here, cols], buf_ref, krow_ref, kcol_ref, eye_ref, p, q
                )
            return 0

        lax.fori_loop(0, QB, column, 0)

    return pl.pallas_call(
        kernel,
        out_shape=jax.ShapeDtypeStruct(front_orig.shape, jnp.bfloat16),
        in_specs=[pl.BlockSpec(memory_space=SMEM)] * 2
        + [pl.BlockSpec(memory_space=pl.ANY)] * 16
        + [pl.BlockSpec(memory_space=VMEM)],
        out_specs=pl.BlockSpec(memory_space=VMEM),
        scratch_shapes=[
            pltpu.VMEM((32, block, 4 * block), jnp.bfloat16),
            pltpu.VMEM((4, block, 2 * block), jnp.bfloat16),
            pltpu.SemaphoreType.DMA((16,)),
        ],
        compiler_params=params(63),
        name="assemble",
    )(krow, kcol, *arrived, front_orig)


def finish(pos, front, row_panel, pieces):
    _, cols = front.shape
    wide = cols // 4

    def kernel(pos_ref, front_ref, row_ref, p0, p1, p2, p3, out_ref):
        zk = pos_ref[0] % 4
        for w, ref in enumerate((p0, p1, p2, p3)):
            here = pl.ds(pl.multiple_of((zk ^ w) * wide, wide), wide)
            update = lax.dot_general(
                row_ref[...], ref[...], (((1,), (1,)), ((), ())), preferred_element_type=jnp.float32
            )
            out_ref[:, here] = (front_ref[:, here].astype(jnp.float32) - update).astype(jnp.bfloat16)

    return pl.pallas_call(
        kernel,
        out_shape=jax.ShapeDtypeStruct(front.shape, jnp.bfloat16),
        in_specs=[pl.BlockSpec(memory_space=SMEM)] + [pl.BlockSpec(memory_space=VMEM)] * 6,
        out_specs=pl.BlockSpec(memory_space=VMEM),
        compiler_params=params(63),
        name="finish",
    )(pos, front, row_panel, *pieces)


def device(x, z, core, y):
    return ((x * 2 + z) * 2 + core) * 4 + y


def moved(array, pairs):
    return lax.ppermute(array, ("x", "z", "core", "col"), pairs)


def over_zk(array, d):
    return lax.ppermute(array, ("z", "core"), [(r, r ^ d) for r in range(4)])


def local(front_orig, child_updates, child_map, panel_inverse):
    me_x = lax.axis_index("x")
    me_z = lax.axis_index("z")
    me_core = lax.axis_index("core")
    me_col = lax.axis_index("col")
    pos = jnp.stack([me_x * 4 + me_z * 2 + me_core, me_col]).astype(jnp.int32)
    other = over_zk(child_updates, 1)
    sel, jsel, jl, krow, kcol = tables(child_map, pos)

    arrived = []
    for chunk in range(4):
        sent = pack_first(sel, jsel, pos, child_updates, other, chunk)
        part = lax.all_to_all(sent, ("x", "col"), 0, 0, tiled=True)
        out = pack_second(jl, pos, part)
        arrived += [out[0]] + [over_zk(out[d], d) for d in (1, 2, 3)]
    first = arrived[:8]

    panel_0 = strip_panel(krow, kcol, first, front_orig, panel_inverse)
    spread = [
        moved(panel_0, [(device(x, z, k, 0), device(x, z, k, y)) for x, z, k in PLACES])
        for y in range(1, 4)
    ]
    sides = [
        moved(panel_0, [(device(x, z, k, 0), device((x + d) % 4, z, k, x)) for x, z, k in PLACES])
        for d in range(1, 4)
    ]
    row_panel = jnp.where(me_col == 0, panel_0, spread[0] + spread[1] + spread[2])
    piece = jnp.where(me_x == me_col, row_panel, sides[0] + sides[1] + sides[2])
    across = over_zk(piece, 2)
    pieces = [piece, over_zk(piece, 1), across, over_zk(across, 1)]

    front = assemble(krow, kcol, arrived, front_orig)
    return (finish(pos, front, row_panel, pieces), row_panel)


def solution(mesh):
    rows = ("hyp", "x", "z", "core")
    split = Mesh(mesh.devices.reshape(-1, 4, 2, 2, 4), rows + ("col",))
    in_specs = (P(rows, "col"), P(rows, "col"), P("hyp", None), P("hyp", None))
    out_specs = (P(rows, "col"), P(rows, None))
    return jax.shard_map(local, mesh=split, in_specs=in_specs, out_specs=out_specs, check_vma=False)
```

```python
import jax
import jax.numpy as jnp
from jax import lax
from jax.experimental import pallas as pl
from jax.experimental.pallas import tpu as pltpu
from jax.sharding import Mesh, PartitionSpec as P


SMEM = pltpu.MemorySpace.SMEM
VMEM = pltpu.MemorySpace.VMEM
CB = 64
MB = 5
QB = 20
FB = 80
CHUNKS = ((0, 0, 1), (0, 1, 2), (1, 0, 2))
PLACES = [(x, z, core) for x in range(4) for z in range(2) for core in range(2)]


def params(mib):
    return pltpu.CompilerParams(vmem_limit_bytes=mib << 20)


def tables_kernel(map_ref, pos_ref, sel_ref, jsel_ref, jl_ref, krow_ref, kcol_ref, inv_ref, cnt_ref):
    row = pos_ref[0]
    col = pos_ref[1]
    x = row // 4
    zk = row % 4
    child = row // 8
    group = (row % 8) // 2

    def clear(i, _):
        inv_ref[i] = -1
        return 0

    lax.fori_loop(0, 2 * FB, clear, 0, unroll=8)
    for c in range(2):

        def invert(i, _):
            inv_ref[c * FB + map_ref[c, i]] = i
            return 0

        lax.fori_loop(0, CB, invert, 0, unroll=8)
    for y in range(4):

        def pick(q, counts):
            v = inv_ref[child * FB + y * QB + q]
            hit = jnp.logical_and(v >= 0, v // 16 == group)
            sel_ref[jnp.where(hit, y * 4 + counts[0], 16)] = v % 16
            hit_j = jnp.logical_and(v >= 0, v // 16 == col)
            jsel_ref[jnp.where(hit_j, y * 4 + counts[1], 16)] = v % 16
            return counts[0] + hit.astype(jnp.int32), counts[1] + hit_j.astype(jnp.int32)

        lax.fori_loop(0, QB, pick, (jnp.int32(0), jnp.int32(0)))
    for c in range(2):
        count = 0
        for p in range(MB):
            hit = inv_ref[c * FB + row * MB + p] >= 0
            krow_ref[c * MB + p] = jnp.where(hit, count, -1)
            count = count + hit.astype(jnp.int32)
        for g in range(10):
            cnt_ref[g] = 0

        def arrive(q, _):
            v = inv_ref[c * FB + col * QB + q]
            hit = v >= 0
            g = jnp.where(hit, v // 16, 4)
            rank = cnt_ref[g]
            cnt_ref[g] = rank + 1
            sender = ((g % 2) * 2 + rank % 2) ^ zk
            kcol_ref[c * QB + q] = jnp.where(hit, ((rank // 2) * 4 + sender) * 4 + c * 2 + g // 2, -1)
            return 0

        lax.fori_loop(0, QB, arrive, 0)
        for d in range(4):

            def pass_on(q, count):
                v = inv_ref[c * FB + x * QB + d * MB + q]
                hit = v >= 0
                g = jnp.where(hit, v // 16, 4)
                slot = cnt_ref[5 + g]
                cnt_ref[5 + g] = slot + 1
                jl_ref[jnp.where(hit, c * 16 + d * 4 + count, 32)] = g * 4 + slot
                return count + hit.astype(jnp.int32)

            lax.fori_loop(0, MB, pass_on, jnp.int32(0))


def tables(child_map, pos):
    shapes = [32, 32, 48, 16, 48]
    return pl.pallas_call(
        tables_kernel,
        out_shape=[jax.ShapeDtypeStruct((n,), jnp.int32) for n in shapes],
        in_specs=[pl.BlockSpec(memory_space=SMEM)] * 2,
        out_specs=[pl.BlockSpec(memory_space=SMEM)] * 5,
        scratch_shapes=[pltpu.SMEM((2 * FB,), jnp.int32), pltpu.SMEM((16,), jnp.int32)],
        compiler_params=params(63),
        name="tables",
    )(child_map, pos)


def pack_first(sel, jsel, pos, own, other, chunk):
    block = own.shape[0] // 8
    turn, first, last = (n * block // 2 if i else n for i, n in enumerate(CHUNKS[chunk]))

    def kernel(sel_ref, jsel_ref, pos_ref, own_ref, other_ref, out_ref, sem):
        core = pos_ref[0] % 2
        for y in range(4):
            index = sel_ref[y * 4 + 2 * turn + core]
            rows = pl.ds(pl.multiple_of((index % 8) * block + first, block // 2), last - first)
            mine = index // 8 == core

            def copy(ref):
                for x in range(4):
                    for k in range(4):
                        cols = pl.ds(pl.multiple_of(jsel_ref[x * 4 + k] * block, block), block)
                        pltpu.make_async_copy(
                            ref.at[rows, cols],
                            out_ref.at[x * 4 + y, :, pl.ds(k * block, block)],
                            sem,
                        ).start()

            pl.when(mine)(lambda: copy(own_ref))
            pl.when(jnp.logical_not(mine))(lambda: copy(other_ref))

        pltpu.make_async_copy(out_ref, out_ref, sem).wait()

    return pl.pallas_call(
        kernel,
        out_shape=jax.ShapeDtypeStruct((16, last - first, 4 * block), own.dtype),
        in_specs=[pl.BlockSpec(memory_space=SMEM)] * 3 + [pl.BlockSpec(memory_space=pltpu.MemorySpace.HBM)] * 2,
        out_specs=pl.BlockSpec(memory_space=VMEM),
        scratch_shapes=[pltpu.SemaphoreType.DMA(())],
        compiler_params=params(63),
    )(sel, jsel, pos, own, other)


def pack_second(jl, pos, arrived):
    block = arrived.shape[2] // 4

    def kernel(jl_ref, pos_ref, in_ref, *out_refs):
        zk = pos_ref[0] % 4
        for d in range(4):
            for xs in range(4):
                for k in range(4):
                    code = jl_ref[(xs // 2) * 16 + (zk ^ d) * 4 + k]
                    cols = pl.ds(pl.multiple_of((code % 4) * block, block), block)
                    out_refs[min(d, 2)][xs + 4 * (d == 3), :, k * block : (k + 1) * block] = in_ref[
                        xs * 4 + code // 4, :, cols
                    ]

    return pl.pallas_call(
        kernel,
        out_shape=[
            jax.ShapeDtypeStruct((n,) + arrived.shape[1:], arrived.dtype) for n in (4, 4, 8)
        ],
        in_specs=[pl.BlockSpec(memory_space=SMEM)] * 2 + [pl.BlockSpec(memory_space=VMEM)],
        out_specs=[pl.BlockSpec(memory_space=VMEM)] * 3,
        compiler_params=params(63),
    )(jl, pos, arrived)


def fill_eyes(eye_ref):
    block = eye_ref.shape[1]
    i = lax.broadcasted_iota(jnp.int32, (block, block), 0)
    j = lax.broadcasted_iota(jnp.int32, (block, block), 1)
    eye = (i == j).astype(jnp.float32).astype(jnp.bfloat16)
    zero = jnp.zeros((block, block), jnp.bfloat16)
    for v in range(4):
        eye_ref[v, :, :block] = eye if v & 1 else zero
        eye_ref[v, :, block:] = eye if v & 2 else zero


def front_tile(orig, buf_ref, krow_ref, kcol_ref, eye_ref, p, q):
    block = orig.shape[0]
    parts = []
    bits = 0
    for c in range(2):
        k = krow_ref[c * MB + p]
        e = kcol_ref[c * QB + q]
        bits = bits + jnp.where(jnp.logical_and(k >= 0, e >= 0), 1 << c, 0)
        start = pl.multiple_of(jnp.maximum(k, 0) * block, block)
        parts.append(buf_ref[jnp.maximum(e, 0), :, pl.ds(start, block)])
    both = jnp.concatenate(parts, axis=1)
    added = lax.dot_general(
        eye_ref[bits], both, (((1,), (1,)), ((), ())), preferred_element_type=jnp.float32
    )
    return (orig.astype(jnp.float32) + added).astype(jnp.bfloat16)


def gather(refs, buf_ref, sem, meanwhile):
    half = buf_ref.shape[1] // 2
    copies = []
    for n, ref in enumerate(refs):
        turn, first, last = CHUNKS[n // 4]
        d = n % 4
        source = ref.at[pl.ds(4, 4)] if d == 3 else ref.at[pl.ds(0, 4)]
        target = buf_ref.at[pl.ds(turn * 16 + d * 4, 4), pl.ds(first * half, (last - first) * half)]
        copies.append(pltpu.make_async_copy(source, target, sem.at[n]))
    for copy in copies:
        copy.start()
    meanwhile()
    for copy in copies:
        copy.wait()


def strip_panel(krow, kcol, arrived, front_orig, panel_inverse):
    block = arrived[0].shape[2] // 4
    rows = front_orig.shape[0]

    def kernel(krow_ref, kcol_ref, *refs):
        orig_ref, inverse_ref, out_ref, buf_ref, eye_ref, sem = refs[8:]
        gather(refs[:8], buf_ref, sem, lambda: fill_eyes(eye_ref))
        for p in range(MB):
            here = slice(p * block, (p + 1) * block)
            tiles = [
                front_tile(
                    orig_ref[here, q * block : (q + 1) * block],
                    buf_ref, krow_ref, kcol_ref, eye_ref, p, q,
                )
                for q in range(2)
            ]
            out_ref[here, :] = jnp.dot(
                jnp.concatenate(tiles, axis=1), inverse_ref[...], preferred_element_type=jnp.float32
            ).astype(jnp.bfloat16)

    return pl.pallas_call(
        kernel,
        grid=(1,),
        out_shape=jax.ShapeDtypeStruct((rows, 2 * block), jnp.bfloat16),
        in_specs=[pl.BlockSpec(memory_space=SMEM)] * 2
        + [pl.BlockSpec(memory_space=pl.ANY)] * 8
        + [
            pl.BlockSpec((rows, 2 * block), lambda i: (0, 0)),
            pl.BlockSpec(memory_space=VMEM),
        ],
        out_specs=pl.BlockSpec(memory_space=VMEM),
        scratch_shapes=[
            pltpu.VMEM((16, block, 4 * block), jnp.bfloat16),
            pltpu.VMEM((4, block, 2 * block), jnp.bfloat16),
            pltpu.SemaphoreType.DMA((8,)),
        ],
        compiler_params=params(63),
        name="strip_panel",
    )(krow, kcol, *arrived, front_orig, panel_inverse)


def assemble(krow, kcol, arrived, front_orig):
    block = arrived[0].shape[2] // 4
    rows, cols = front_orig.shape

    def kernel(krow_ref, kcol_ref, *refs):
        orig_ref, out_ref, buf_ref, eye_ref, sem = refs[12:]
        step = pl.program_id(0)

        @pl.when(step == 0)
        def _():
            gather(refs[:12], buf_ref, sem, lambda: fill_eyes(eye_ref))

        for q in range(QB // 4):
            side = slice(q * block, (q + 1) * block)
            for p in range(MB):
                here = slice(p * block, (p + 1) * block)
                out_ref[here, side] = front_tile(
                    orig_ref[here, side], buf_ref, krow_ref, kcol_ref, eye_ref, p, step * (QB // 4) + q
                )

    return pl.pallas_call(
        kernel,
        grid=(4,),
        out_shape=jax.ShapeDtypeStruct(front_orig.shape, jnp.bfloat16),
        in_specs=[pl.BlockSpec(memory_space=SMEM)] * 2
        + [pl.BlockSpec(memory_space=pl.ANY)] * 12
        + [pl.BlockSpec((rows, cols // 4), lambda i: (0, i))],
        out_specs=pl.BlockSpec((rows, cols // 4), lambda i: (0, i)),
        scratch_shapes=[
            pltpu.VMEM((32, block, 4 * block), jnp.bfloat16),
            pltpu.VMEM((4, block, 2 * block), jnp.bfloat16),
            pltpu.SemaphoreType.DMA((12,)),
        ],
        compiler_params=params(63),
        name="assemble",
    )(krow, kcol, *arrived, front_orig)


def finish(pos, front, row_panel, pieces):
    rows, cols = front.shape
    wide = cols // 4

    def kernel(pos_ref, front_ref, row_ref, *refs):
        out_ref = refs[4]
        for w in range(4):

            @pl.when(pl.program_id(0) == w)
            def _():
                update = lax.dot_general(
                    row_ref[...], refs[w][...], (((1,), (1,)), ((), ())),
                    preferred_element_type=jnp.float32,
                )
                out_ref[...] = (front_ref[...].astype(jnp.float32) - update).astype(jnp.bfloat16)

    whole = pl.BlockSpec(row_panel.shape, lambda w, pos_ref: (0, 0))
    turned = pl.BlockSpec((rows, wide), lambda w, pos_ref: (0, (pos_ref[0] % 4) ^ w))
    return pl.pallas_call(
        kernel,
        grid_spec=pltpu.PrefetchScalarGridSpec(
            num_scalar_prefetch=1,
            grid=(4,),
            in_specs=[turned] + [whole] * 5,
            out_specs=turned,
        ),
        out_shape=jax.ShapeDtypeStruct(front.shape, jnp.bfloat16),
        compiler_params=params(63),
        name="finish",
    )(pos, front, row_panel, *pieces)


def device(x, z, core, y):
    return ((x * 2 + z) * 2 + core) * 4 + y


def moved(array, pairs):
    return lax.ppermute(array, ("x", "z", "core", "col"), pairs)


def over_zk(array, d):
    return lax.ppermute(array, ("z", "core"), [(r, r ^ d) for r in range(4)])


def local(front_orig, child_updates, child_map, panel_inverse):
    me_x = lax.axis_index("x")
    me_z = lax.axis_index("z")
    me_core = lax.axis_index("core")
    me_col = lax.axis_index("col")
    pos = jnp.stack([me_x * 4 + me_z * 2 + me_core, me_col]).astype(jnp.int32)
    other = over_zk(child_updates, 1)
    sel, jsel, jl, krow, kcol = tables(child_map, pos)

    arrived = []
    for chunk in range(len(CHUNKS)):
        sent = pack_first(sel, jsel, pos, child_updates, other, chunk)
        part = lax.all_to_all(sent, ("x", "col"), 0, 0, tiled=True)
        stay, swap, out = pack_second(jl, pos, part)
        crossed = over_zk(out, 2)
        arrived += [stay, over_zk(swap, 1), crossed, over_zk(crossed, 1)]
    first = arrived[:8]

    panel_0 = strip_panel(krow, kcol, first, front_orig, panel_inverse)
    spread = [
        moved(panel_0, [(device(x, z, k, 0), device(x, z, k, y)) for x, z, k in PLACES])
        for y in range(1, 4)
    ]
    sides = [
        moved(panel_0, [(device(x, z, k, 0), device((x + d) % 4, z, k, x)) for x, z, k in PLACES])
        for d in range(1, 4)
    ]
    row_panel = jnp.where(me_col == 0, panel_0, spread[0] + spread[1] + spread[2])
    piece = jnp.where(me_x == me_col, row_panel, sides[0] + sides[1] + sides[2])
    across = over_zk(piece, 2)
    pieces = [piece, over_zk(piece, 1), across, over_zk(across, 1)]

    front = assemble(krow, kcol, arrived, front_orig)
    return (finish(pos, front, row_panel, pieces), row_panel)


def solution(mesh):
    rows = ("hyp", "x", "z", "core")
    split = Mesh(mesh.devices.reshape(-1, 4, 2, 2, 4), rows + ("col",))
    in_specs = (P(rows, "col"), P(rows, "col"), P("hyp", None), P("hyp", None))
    out_specs = (P(rows, "col"), P(rows, None))
    return jax.shard_map(local, mesh=split, in_specs=in_specs, out_specs=out_specs, check_vma=False)
```

```python
import jax
import jax.numpy as jnp
from jax import lax
from jax.experimental import pallas as pl
from jax.experimental.pallas import tpu as pltpu
from jax.sharding import Mesh, PartitionSpec as P


SMEM = pltpu.MemorySpace.SMEM
VMEM = pltpu.MemorySpace.VMEM
CB = 64
MB = 5
QB = 20
FB = 80
CHUNKS = ((0, 0, 1), (0, 1, 2), (1, 0, 2))
PLACES = [(x, z, core) for x in range(4) for z in range(2) for core in range(2)]


def params(mib):
    return pltpu.CompilerParams(vmem_limit_bytes=mib << 20)


def tables_kernel(map_ref, pos_ref, sel_ref, jsel_ref, jl_ref, krow_ref, kcol_ref, inv_ref, cnt_ref):
    row = pos_ref[0]
    col = pos_ref[1]
    x = row // 4
    zk = row % 4
    child = row // 8
    group = (row % 8) // 2

    def clear(i, _):
        inv_ref[i] = -1
        return 0

    lax.fori_loop(0, 2 * FB, clear, 0, unroll=8)
    for c in range(2):

        def invert(i, _):
            inv_ref[c * FB + map_ref[c, i]] = i
            return 0

        lax.fori_loop(0, CB, invert, 0, unroll=8)
    for y in range(4):

        def pick(q, counts):
            v = inv_ref[child * FB + y * QB + q]
            hit = jnp.logical_and(v >= 0, v // 16 == group)
            sel_ref[jnp.where(hit, y * 4 + counts[0], 16)] = v % 16
            hit_j = jnp.logical_and(v >= 0, v // 16 == col)
            jsel_ref[jnp.where(hit_j, y * 4 + counts[1], 16)] = v % 16
            return counts[0] + hit.astype(jnp.int32), counts[1] + hit_j.astype(jnp.int32)

        lax.fori_loop(0, QB, pick, (jnp.int32(0), jnp.int32(0)))
    for c in range(2):
        count = 0
        for p in range(MB):
            hit = inv_ref[c * FB + row * MB + p] >= 0
            krow_ref[c * MB + p] = jnp.where(hit, count, -1)
            count = count + hit.astype(jnp.int32)
        for g in range(10):
            cnt_ref[g] = 0

        def arrive(q, _):
            v = inv_ref[c * FB + col * QB + q]
            hit = v >= 0
            g = jnp.where(hit, v // 16, 4)
            rank = cnt_ref[g]
            cnt_ref[g] = rank + 1
            sender = ((g % 2) * 2 + rank % 2) ^ zk
            kcol_ref[c * QB + q] = jnp.where(hit, ((rank // 2) * 4 + sender) * 4 + c * 2 + g // 2, -1)
            return 0

        lax.fori_loop(0, QB, arrive, 0)
        for d in range(4):

            def pass_on(q, count):
                v = inv_ref[c * FB + x * QB + d * MB + q]
                hit = v >= 0
                g = jnp.where(hit, v // 16, 4)
                slot = cnt_ref[5 + g]
                cnt_ref[5 + g] = slot + 1
                jl_ref[jnp.where(hit, c * 16 + d * 4 + count, 32)] = g * 4 + slot
                return count + hit.astype(jnp.int32)

            lax.fori_loop(0, MB, pass_on, jnp.int32(0))


def tables(child_map, pos):
    shapes = [32, 32, 48, 16, 48]
    return pl.pallas_call(
        tables_kernel,
        out_shape=[jax.ShapeDtypeStruct((n,), jnp.int32) for n in shapes],
        in_specs=[pl.BlockSpec(memory_space=SMEM)] * 2,
        out_specs=[pl.BlockSpec(memory_space=SMEM)] * 5,
        scratch_shapes=[pltpu.SMEM((2 * FB,), jnp.int32), pltpu.SMEM((16,), jnp.int32)],
        compiler_params=params(63),
        name="tables",
    )(child_map, pos)


def pack_first(sel, jsel, pos, own, other, chunk):
    block = own.shape[0] // 8
    turn, first, last = (n * block // 2 if i else n for i, n in enumerate(CHUNKS[chunk]))

    def kernel(sel_ref, jsel_ref, pos_ref, own_ref, other_ref, out_ref, sem):
        core = pos_ref[0] % 2
        for y in range(4):
            index = sel_ref[y * 4 + 2 * turn + core]
            rows = pl.ds(pl.multiple_of((index % 8) * block + first, block // 2), last - first)
            mine = index // 8 == core

            def copy(ref):
                for x in range(4):
                    for k in range(4):
                        cols = pl.ds(pl.multiple_of(jsel_ref[x * 4 + k] * block, block), block)
                        pltpu.make_async_copy(
                            ref.at[rows, cols],
                            out_ref.at[x * 4 + y, :, pl.ds(k * block, block)],
                            sem,
                        ).start()

            pl.when(mine)(lambda: copy(own_ref))
            pl.when(jnp.logical_not(mine))(lambda: copy(other_ref))

        pltpu.make_async_copy(out_ref, out_ref, sem).wait()

    return pl.pallas_call(
        kernel,
        out_shape=jax.ShapeDtypeStruct((16, last - first, 4 * block), own.dtype),
        in_specs=[pl.BlockSpec(memory_space=SMEM)] * 3 + [pl.BlockSpec(memory_space=pltpu.MemorySpace.HBM)] * 2,
        out_specs=pl.BlockSpec(memory_space=VMEM),
        scratch_shapes=[pltpu.SemaphoreType.DMA(())],
        compiler_params=params(63),
    )(sel, jsel, pos, own, other)


def pack_second(jl, pos, arrived):
    block = arrived.shape[2] // 4

    def kernel(jl_ref, pos_ref, in_ref, *out_refs):
        zk = pos_ref[0] % 4
        for d in range(4):
            for xs in range(4):
                for k in range(4):
                    code = jl_ref[(xs // 2) * 16 + (zk ^ d) * 4 + k]
                    cols = pl.ds(pl.multiple_of((code % 4) * block, block), block)
                    out_refs[min(d, 2)][xs + 4 * (d == 3), :, k * block : (k + 1) * block] = in_ref[
                        xs * 4 + code // 4, :, cols
                    ]

    return pl.pallas_call(
        kernel,
        out_shape=[
            jax.ShapeDtypeStruct((n,) + arrived.shape[1:], arrived.dtype) for n in (4, 4, 8)
        ],
        in_specs=[pl.BlockSpec(memory_space=SMEM)] * 2 + [pl.BlockSpec(memory_space=VMEM)],
        out_specs=[pl.BlockSpec(memory_space=VMEM)] * 3,
        compiler_params=params(63),
    )(jl, pos, arrived)


def fill_eyes(eye_ref):
    block = eye_ref.shape[1]
    i = lax.broadcasted_iota(jnp.int32, (block, block), 0)
    j = lax.broadcasted_iota(jnp.int32, (block, block), 1)
    eye = (i == j).astype(jnp.float32).astype(jnp.bfloat16)
    zero = jnp.zeros((block, block), jnp.bfloat16)
    for v in range(4):
        eye_ref[v, :, :block] = eye if v & 1 else zero
        eye_ref[v, :, block:] = eye if v & 2 else zero


def front_tile(orig, buf_ref, krow_ref, kcol_ref, eye_ref, p, q):
    block = orig.shape[0]
    parts = []
    bits = 0
    for c in range(2):
        k = krow_ref[c * MB + p]
        e = kcol_ref[c * QB + q]
        bits = bits + jnp.where(jnp.logical_and(k >= 0, e >= 0), 1 << c, 0)
        start = pl.multiple_of(jnp.maximum(k, 0) * block, block)
        parts.append(buf_ref[jnp.maximum(e, 0), :, pl.ds(start, block)])
    both = jnp.concatenate(parts, axis=1)
    added = lax.dot_general(
        eye_ref[bits], both, (((1,), (1,)), ((), ())), preferred_element_type=jnp.float32
    )
    return (orig.astype(jnp.float32) + added).astype(jnp.bfloat16)


def gather(refs, buf_ref, sem, meanwhile):
    half = buf_ref.shape[1] // 2
    copies = []
    for n, ref in enumerate(refs):
        turn, first, last = CHUNKS[n // 4]
        d = n % 4
        source = ref.at[pl.ds(4, 4)] if d == 3 else ref.at[pl.ds(0, 4)]
        target = buf_ref.at[pl.ds(turn * 16 + d * 4, 4), pl.ds(first * half, (last - first) * half)]
        copies.append(pltpu.make_async_copy(source, target, sem.at[n]))
    for copy in copies:
        copy.start()
    meanwhile()
    for copy in copies:
        copy.wait()


def strip_panel(krow, kcol, arrived, front_orig, panel_inverse):
    block = arrived[0].shape[2] // 4
    rows = front_orig.shape[0]

    def kernel(krow_ref, kcol_ref, *refs):
        orig_ref, inverse_ref, out_ref, buf_ref, eye_ref, sem = refs[8:]
        gather(refs[:8], buf_ref, sem, lambda: fill_eyes(eye_ref))
        for p in range(MB):
            here = slice(p * block, (p + 1) * block)
            tiles = [
                front_tile(
                    orig_ref[here, q * block : (q + 1) * block],
                    buf_ref, krow_ref, kcol_ref, eye_ref, p, q,
                )
                for q in range(2)
            ]
            out_ref[here, :] = jnp.dot(
                jnp.concatenate(tiles, axis=1), inverse_ref[...], preferred_element_type=jnp.float32
            ).astype(jnp.bfloat16)

    return pl.pallas_call(
        kernel,
        grid=(1,),
        out_shape=jax.ShapeDtypeStruct((rows, 2 * block), jnp.bfloat16),
        in_specs=[pl.BlockSpec(memory_space=SMEM)] * 2
        + [pl.BlockSpec(memory_space=pl.ANY)] * 8
        + [
            pl.BlockSpec((rows, 2 * block), lambda i: (0, 0)),
            pl.BlockSpec(memory_space=VMEM),
        ],
        out_specs=pl.BlockSpec(memory_space=VMEM),
        scratch_shapes=[
            pltpu.VMEM((16, block, 4 * block), jnp.bfloat16),
            pltpu.VMEM((4, block, 2 * block), jnp.bfloat16),
            pltpu.SemaphoreType.DMA((8,)),
        ],
        compiler_params=params(63),
        name="strip_panel",
    )(krow, kcol, *arrived, front_orig, panel_inverse)


def assemble(pos, krow, kcol, arrived, front_orig, row_panel, pieces):
    block = arrived[0].shape[2] // 4
    rows, cols = front_orig.shape

    def kernel(pos_ref, krow_ref, kcol_ref, *refs):
        orig_ref, row_ref, own_ref, twin_ref, out_ref, buf_ref, eye_ref, sem = refs[12:]
        step = pl.program_id(0)
        first = ((pos_ref[0] % 4) ^ step) * (QB // 4)

        @pl.when(step == 0)
        def _():
            gather(refs[:12], buf_ref, sem, lambda: fill_eyes(eye_ref))

        for q in range(QB // 4):
            side = slice(q * block, (q + 1) * block)
            for p in range(MB):
                here = slice(p * block, (p + 1) * block)
                out_ref[here, side] = front_tile(
                    orig_ref[here, side], buf_ref, krow_ref, kcol_ref, eye_ref, p, first + q
                )
        for w, ref in enumerate((own_ref, twin_ref)):

            @pl.when(step == w)
            def _():
                subtract(out_ref, out_ref, row_ref, ref)

    whole = pl.BlockSpec(row_panel.shape, lambda w, pos_ref: (0, 0))
    turned = pl.BlockSpec((rows, cols // 4), lambda w, pos_ref: (0, (pos_ref[0] % 4) ^ w))
    return pl.pallas_call(
        kernel,
        grid_spec=pltpu.PrefetchScalarGridSpec(
            num_scalar_prefetch=1,
            grid=(4,),
            in_specs=[pl.BlockSpec(memory_space=SMEM)] * 2
            + [pl.BlockSpec(memory_space=pl.ANY)] * 12
            + [turned]
            + [whole] * 3,
            out_specs=turned,
            scratch_shapes=[
                pltpu.VMEM((32, block, 4 * block), jnp.bfloat16),
                pltpu.VMEM((4, block, 2 * block), jnp.bfloat16),
                pltpu.SemaphoreType.DMA((12,)),
            ],
        ),
        out_shape=jax.ShapeDtypeStruct(front_orig.shape, jnp.bfloat16),
        compiler_params=params(63),
        name="assemble",
    )(pos, krow, kcol, *arrived, front_orig, row_panel, *pieces)


def subtract(out_ref, front_ref, row_ref, piece_ref):
    update = lax.dot_general(
        row_ref[...], piece_ref[...], (((1,), (1,)), ((), ())), preferred_element_type=jnp.float32
    )
    out_ref[...] = (front_ref[...].astype(jnp.float32) - update).astype(jnp.bfloat16)


def finish(pos, front, row_panel, pieces):
    rows, cols = front.shape

    def kernel(pos_ref, front_ref, row_ref, own_ref, twin_ref, out_ref):
        for w, ref in enumerate((own_ref, twin_ref)):

            @pl.when(pl.program_id(0) == w)
            def _():
                subtract(out_ref, front_ref, row_ref, ref)

    whole = pl.BlockSpec(row_panel.shape, lambda w, pos_ref: (0, 0))
    turned = pl.BlockSpec((rows, cols // 4), lambda w, pos_ref: (0, (pos_ref[0] % 4) ^ (w + 2)))
    return pl.pallas_call(
        kernel,
        grid_spec=pltpu.PrefetchScalarGridSpec(
            num_scalar_prefetch=1,
            grid=(2,),
            in_specs=[turned] + [whole] * 3,
            out_specs=turned,
        ),
        out_shape=jax.ShapeDtypeStruct(front.shape, jnp.bfloat16),
        input_output_aliases={1: 0},
        compiler_params=params(63),
        name="finish",
    )(pos, front, row_panel, *pieces)


def device(x, z, core, y):
    return ((x * 2 + z) * 2 + core) * 4 + y


def moved(array, pairs):
    return lax.ppermute(array, ("x", "z", "core", "col"), pairs)


def over_zk(array, d):
    return lax.ppermute(array, ("z", "core"), [(r, r ^ d) for r in range(4)])


def local(front_orig, child_updates, child_map, panel_inverse):
    me_x = lax.axis_index("x")
    me_z = lax.axis_index("z")
    me_core = lax.axis_index("core")
    me_col = lax.axis_index("col")
    pos = jnp.stack([me_x * 4 + me_z * 2 + me_core, me_col]).astype(jnp.int32)
    other = over_zk(child_updates, 1)
    sel, jsel, jl, krow, kcol = tables(child_map, pos)

    arrived = []
    for chunk in range(len(CHUNKS)):
        sent = pack_first(sel, jsel, pos, child_updates, other, chunk)
        part = lax.all_to_all(sent, ("x", "col"), 0, 0, tiled=True)
        stay, swap, out = pack_second(jl, pos, part)
        crossed = over_zk(out, 2)
        near = over_zk(swap, 1)
        arrived += [stay, near, crossed, over_zk(crossed, 1)]
    first = arrived[:8]

    panel_0 = strip_panel(krow, kcol, first, front_orig, panel_inverse)
    spread = [
        moved(panel_0, [(device(x, z, k, 0), device(x, z, k, y)) for x, z, k in PLACES])
        for y in range(1, 4)
    ]
    sides = [
        moved(panel_0, [(device(x, z, k, 0), device((x + d) % 4, z, k, x)) for x, z, k in PLACES])
        for d in range(1, 4)
    ]
    row_panel = jnp.where(me_col == 0, panel_0, spread[0] + spread[1] + spread[2])
    piece = jnp.where(me_x == me_col, row_panel, sides[0] + sides[1] + sides[2])
    across = over_zk(piece, 2)
    near = [piece, over_zk(piece, 1)]
    far = [across, over_zk(across, 1)]
    front = assemble(pos, krow, kcol, arrived, front_orig, row_panel, near)
    return (finish(pos, front, row_panel, far), row_panel)


def solution(mesh):
    rows = ("hyp", "x", "z", "core")
    split = Mesh(mesh.devices.reshape(-1, 4, 2, 2, 4), rows + ("col",))
    in_specs = (P(rows, "col"), P(rows, "col"), P("hyp", None), P("hyp", None))
    out_specs = (P(rows, "col"), P(rows, None))
    return jax.shard_map(local, mesh=split, in_specs=in_specs, out_specs=out_specs, check_vma=False)
```

```python
import jax
import jax.numpy as jnp
from jax import lax
from jax.experimental import pallas as pl
from jax.experimental.pallas import tpu as pltpu
from jax.sharding import Mesh, PartitionSpec as P


SMEM = pltpu.MemorySpace.SMEM
VMEM = pltpu.MemorySpace.VMEM
CB = 64
MB = 5
QB = 20
FB = 80
CHUNKS = ((0, 0, 1), (0, 1, 2), (1, 0, 1), (1, 1, 2))
PLACES = [(x, z, core) for x in range(4) for z in range(2) for core in range(2)]


def params(mib):
    return pltpu.CompilerParams(vmem_limit_bytes=mib << 20)


def tables_kernel(map_ref, pos_ref, sel_ref, jsel_ref, jl_ref, krow_ref, kcol_ref, inv_ref, cnt_ref):
    row = pos_ref[0]
    col = pos_ref[1]
    x = row // 4
    zk = row % 4
    child = row // 8
    group = (row % 8) // 2

    def clear(i, _):
        inv_ref[i] = -1
        return 0

    lax.fori_loop(0, 2 * FB, clear, 0, unroll=8)
    for c in range(2):

        def invert(i, _):
            inv_ref[c * FB + map_ref[c, i]] = i
            return 0

        lax.fori_loop(0, CB, invert, 0, unroll=8)
    for y in range(4):

        def pick(q, counts):
            v = inv_ref[child * FB + y * QB + q]
            hit = jnp.logical_and(v >= 0, v // 16 == group)
            sel_ref[jnp.where(hit, y * 4 + counts[0], 16)] = v % 16
            hit_j = jnp.logical_and(v >= 0, v // 16 == col)
            jsel_ref[jnp.where(hit_j, y * 4 + counts[1], 16)] = v % 16
            return counts[0] + hit.astype(jnp.int32), counts[1] + hit_j.astype(jnp.int32)

        lax.fori_loop(0, QB, pick, (jnp.int32(0), jnp.int32(0)))
    for c in range(2):
        count = 0
        for p in range(MB):
            hit = inv_ref[c * FB + row * MB + p] >= 0
            krow_ref[c * MB + p] = jnp.where(hit, count, -1)
            count = count + hit.astype(jnp.int32)
        for g in range(10):
            cnt_ref[g] = 0

        def arrive(q, _):
            v = inv_ref[c * FB + col * QB + q]
            hit = v >= 0
            g = jnp.where(hit, v // 16, 4)
            rank = cnt_ref[g]
            cnt_ref[g] = rank + 1
            sender = ((g % 2) * 2 + rank % 2) ^ zk
            kcol_ref[c * QB + q] = jnp.where(hit, ((rank // 2) * 4 + sender) * 4 + c * 2 + g // 2, -1)
            return 0

        lax.fori_loop(0, QB, arrive, 0)
        for d in range(4):

            def pass_on(q, count):
                v = inv_ref[c * FB + x * QB + d * MB + q]
                hit = v >= 0
                g = jnp.where(hit, v // 16, 4)
                slot = cnt_ref[5 + g]
                cnt_ref[5 + g] = slot + 1
                jl_ref[jnp.where(hit, c * 16 + d * 4 + count, 32)] = g * 4 + slot
                return count + hit.astype(jnp.int32)

            lax.fori_loop(0, MB, pass_on, jnp.int32(0))


def tables(child_map, pos):
    shapes = [32, 32, 48, 16, 48]
    return pl.pallas_call(
        tables_kernel,
        out_shape=[jax.ShapeDtypeStruct((n,), jnp.int32) for n in shapes],
        in_specs=[pl.BlockSpec(memory_space=SMEM)] * 2,
        out_specs=[pl.BlockSpec(memory_space=SMEM)] * 5,
        scratch_shapes=[pltpu.SMEM((2 * FB,), jnp.int32), pltpu.SMEM((16,), jnp.int32)],
        compiler_params=params(63),
        name="tables",
    )(child_map, pos)


def pack_first(sel, jsel, pos, own, other, chunk):
    block = own.shape[0] // 8
    turn, first, last = (n * block // 2 if i else n for i, n in enumerate(CHUNKS[chunk]))

    def kernel(sel_ref, jsel_ref, pos_ref, own_ref, other_ref, out_ref, sem):
        core = pos_ref[0] % 2
        for y in range(4):
            index = sel_ref[y * 4 + 2 * turn + core]
            rows = pl.ds(pl.multiple_of((index % 8) * block + first, block // 2), last - first)
            mine = index // 8 == core

            def copy(ref):
                for x in range(4):
                    for k in range(4):
                        cols = pl.ds(pl.multiple_of(jsel_ref[x * 4 + k] * block, block), block)
                        pltpu.make_async_copy(
                            ref.at[rows, cols],
                            out_ref.at[x * 4 + y, :, pl.ds(k * block, block)],
                            sem,
                        ).start()

            pl.when(mine)(lambda: copy(own_ref))
            pl.when(jnp.logical_not(mine))(lambda: copy(other_ref))

        pltpu.make_async_copy(out_ref, out_ref, sem).wait()

    return pl.pallas_call(
        kernel,
        out_shape=jax.ShapeDtypeStruct((16, last - first, 4 * block), own.dtype),
        in_specs=[pl.BlockSpec(memory_space=SMEM)] * 3 + [pl.BlockSpec(memory_space=pltpu.MemorySpace.HBM)] * 2,
        out_specs=pl.BlockSpec(memory_space=VMEM),
        scratch_shapes=[pltpu.SemaphoreType.DMA(())],
        compiler_params=params(63),
    )(sel, jsel, pos, own, other)


def pack_second(jl, pos, arrived):
    block = arrived.shape[2] // 4

    def kernel(jl_ref, pos_ref, in_ref, *out_refs):
        zk = pos_ref[0] % 4
        for d in range(4):
            for xs in range(4):
                for k in range(4):
                    code = jl_ref[(xs // 2) * 16 + (zk ^ d) * 4 + k]
                    cols = pl.ds(pl.multiple_of((code % 4) * block, block), block)
                    out_refs[min(d, 2)][xs + 4 * (d == 3), :, k * block : (k + 1) * block] = in_ref[
                        xs * 4 + code // 4, :, cols
                    ]

    return pl.pallas_call(
        kernel,
        out_shape=[
            jax.ShapeDtypeStruct((n,) + arrived.shape[1:], arrived.dtype) for n in (4, 4, 8)
        ],
        in_specs=[pl.BlockSpec(memory_space=SMEM)] * 2 + [pl.BlockSpec(memory_space=VMEM)],
        out_specs=[pl.BlockSpec(memory_space=VMEM)] * 3,
        compiler_params=params(63),
    )(jl, pos, arrived)


def fill_eyes(eye_ref):
    block = eye_ref.shape[1]
    i = lax.broadcasted_iota(jnp.int32, (block, block), 0)
    j = lax.broadcasted_iota(jnp.int32, (block, block), 1)
    eye = (i == j).astype(jnp.float32).astype(jnp.bfloat16)
    zero = jnp.zeros((block, block), jnp.bfloat16)
    for v in range(4):
        eye_ref[v, :, :block] = eye if v & 1 else zero
        eye_ref[v, :, block:] = eye if v & 2 else zero


def front_tile(orig, buf_ref, krow_ref, kcol_ref, eye_ref, p, q):
    block = orig.shape[0]
    parts = []
    bits = 0
    for c in range(2):
        k = krow_ref[c * MB + p]
        e = kcol_ref[c * QB + q]
        bits = bits + jnp.where(jnp.logical_and(k >= 0, e >= 0), 1 << c, 0)
        start = pl.multiple_of(jnp.maximum(k, 0) * block, block)
        parts.append(buf_ref[jnp.maximum(e, 0), :, pl.ds(start, block)])
    both = jnp.concatenate(parts, axis=1)
    added = lax.dot_general(
        eye_ref[bits], both, (((1,), (1,)), ((), ())), preferred_element_type=jnp.float32
    )
    return (orig.astype(jnp.float32) + added).astype(jnp.bfloat16)


def gather(refs, buf_ref, sem, meanwhile):
    half = buf_ref.shape[1] // 2
    copies = []
    for n, ref in enumerate(refs):
        turn, first, last = CHUNKS[n // 4]
        d = n % 4
        source = ref.at[pl.ds(4, 4)] if d == 3 else ref.at[pl.ds(0, 4)]
        target = buf_ref.at[pl.ds(turn * 16 + d * 4, 4), pl.ds(first * half, (last - first) * half)]
        copies.append(pltpu.make_async_copy(source, target, sem.at[n]))
    for copy in copies:
        copy.start()
    meanwhile()
    for copy in copies:
        copy.wait()


def strip_panel(krow, kcol, arrived, front_orig, panel_inverse):
    block = arrived[0].shape[2] // 4
    rows = front_orig.shape[0]

    def kernel(krow_ref, kcol_ref, *refs):
        orig_ref, inverse_ref, out_ref, buf_ref, eye_ref, sem = refs[8:]
        gather(refs[:8], buf_ref, sem, lambda: fill_eyes(eye_ref))
        for p in range(MB):
            here = slice(p * block, (p + 1) * block)
            tiles = [
                front_tile(
                    orig_ref[here, q * block : (q + 1) * block],
                    buf_ref, krow_ref, kcol_ref, eye_ref, p, q,
                )
                for q in range(2)
            ]
            out_ref[here, :] = jnp.dot(
                jnp.concatenate(tiles, axis=1), inverse_ref[...], preferred_element_type=jnp.float32
            ).astype(jnp.bfloat16)

    return pl.pallas_call(
        kernel,
        grid=(1,),
        out_shape=jax.ShapeDtypeStruct((rows, 2 * block), jnp.bfloat16),
        in_specs=[pl.BlockSpec(memory_space=SMEM)] * 2
        + [pl.BlockSpec(memory_space=pl.ANY)] * 8
        + [
            pl.BlockSpec((rows, 2 * block), lambda i: (0, 0)),
            pl.BlockSpec(memory_space=VMEM),
        ],
        out_specs=pl.BlockSpec(memory_space=VMEM),
        scratch_shapes=[
            pltpu.VMEM((16, block, 4 * block), jnp.bfloat16),
            pltpu.VMEM((4, block, 2 * block), jnp.bfloat16),
            pltpu.SemaphoreType.DMA((8,)),
        ],
        compiler_params=params(63),
        name="strip_panel",
    )(krow, kcol, *arrived, front_orig, panel_inverse)


def assemble(pos, krow, kcol, arrived, front_orig, row_panel, pieces):
    block = arrived[0].shape[2] // 4
    rows, cols = front_orig.shape

    def kernel(pos_ref, krow_ref, kcol_ref, *refs):
        orig_ref, row_ref, own_ref, twin_ref, out_ref, buf_ref, eye_ref, sem = refs[16:]
        step = pl.program_id(0)
        first = ((pos_ref[0] % 4) ^ step) * (QB // 4)

        @pl.when(step == 0)
        def _():
            gather(refs[:16], buf_ref, sem, lambda: fill_eyes(eye_ref))

        for q in range(QB // 4):
            side = slice(q * block, (q + 1) * block)
            for p in range(MB):
                here = slice(p * block, (p + 1) * block)
                out_ref[here, side] = front_tile(
                    orig_ref[here, side], buf_ref, krow_ref, kcol_ref, eye_ref, p, first + q
                )
        for w, ref in enumerate((own_ref, twin_ref)):

            @pl.when(step == w)
            def _():
                subtract(out_ref, out_ref, row_ref, ref)

    whole = pl.BlockSpec(row_panel.shape, lambda w, pos_ref: (0, 0))
    turned = pl.BlockSpec((rows, cols // 4), lambda w, pos_ref: (0, (pos_ref[0] % 4) ^ w))
    return pl.pallas_call(
        kernel,
        grid_spec=pltpu.PrefetchScalarGridSpec(
            num_scalar_prefetch=1,
            grid=(4,),
            in_specs=[pl.BlockSpec(memory_space=SMEM)] * 2
            + [pl.BlockSpec(memory_space=pl.ANY)] * 16
            + [turned]
            + [whole] * 3,
            out_specs=turned,
            scratch_shapes=[
                pltpu.VMEM((32, block, 4 * block), jnp.bfloat16),
                pltpu.VMEM((4, block, 2 * block), jnp.bfloat16),
                pltpu.SemaphoreType.DMA((16,)),
            ],
        ),
        out_shape=jax.ShapeDtypeStruct(front_orig.shape, jnp.bfloat16),
        compiler_params=params(63),
        name="assemble",
    )(pos, krow, kcol, *arrived, front_orig, row_panel, *pieces)


def subtract(out_ref, front_ref, row_ref, piece_ref):
    update = lax.dot_general(
        row_ref[...], piece_ref[...], (((1,), (1,)), ((), ())), preferred_element_type=jnp.float32
    )
    out_ref[...] = (front_ref[...].astype(jnp.float32) - update).astype(jnp.bfloat16)


def finish(pos, front, row_panel, pieces):
    rows, cols = front.shape

    def kernel(pos_ref, front_ref, row_ref, own_ref, twin_ref, out_ref):
        for w, ref in enumerate((own_ref, twin_ref)):

            @pl.when(pl.program_id(0) == w)
            def _():
                subtract(out_ref, front_ref, row_ref, ref)

    whole = pl.BlockSpec(row_panel.shape, lambda w, pos_ref: (0, 0))
    turned = pl.BlockSpec((rows, cols // 4), lambda w, pos_ref: (0, (pos_ref[0] % 4) ^ (w + 2)))
    return pl.pallas_call(
        kernel,
        grid_spec=pltpu.PrefetchScalarGridSpec(
            num_scalar_prefetch=1,
            grid=(2,),
            in_specs=[turned] + [whole] * 3,
            out_specs=turned,
        ),
        out_shape=jax.ShapeDtypeStruct(front.shape, jnp.bfloat16),
        input_output_aliases={1: 0},
        compiler_params=params(63),
        name="finish",
    )(pos, front, row_panel, *pieces)


def device(x, z, core, y):
    return ((x * 2 + z) * 2 + core) * 4 + y


def moved(array, pairs):
    return lax.ppermute(array, ("x", "z", "core", "col"), pairs)


def over_zk(array, d):
    return lax.ppermute(array, ("z", "core"), [(r, r ^ d) for r in range(4)])


def local(front_orig, child_updates, child_map, panel_inverse):
    me_x = lax.axis_index("x")
    me_z = lax.axis_index("z")
    me_core = lax.axis_index("core")
    me_col = lax.axis_index("col")
    pos = jnp.stack([me_x * 4 + me_z * 2 + me_core, me_col]).astype(jnp.int32)
    other = over_zk(child_updates, 1)
    sel, jsel, jl, krow, kcol = tables(child_map, pos)

    arrived = []
    for chunk in range(len(CHUNKS)):
        sent = pack_first(sel, jsel, pos, child_updates, other, chunk)
        part = lax.all_to_all(sent, ("x", "col"), 0, 0, tiled=True)
        stay, swap, out = pack_second(jl, pos, part)
        crossed = over_zk(out, 2)
        near = over_zk(swap, 1)
        arrived += [stay, near, crossed, over_zk(crossed, 1)]
    first = arrived[:8]

    panel_0 = strip_panel(krow, kcol, first, front_orig, panel_inverse)
    spread = [
        moved(panel_0, [(device(x, z, k, 0), device(x, z, k, y)) for x, z, k in PLACES])
        for y in range(1, 4)
    ]
    sides = [
        moved(panel_0, [(device(x, z, k, 0), device((x + d) % 4, z, k, x)) for x, z, k in PLACES])
        for d in range(1, 4)
    ]
    row_panel = jnp.where(me_col == 0, panel_0, spread[0] + spread[1] + spread[2])
    piece = jnp.where(me_x == me_col, row_panel, sides[0] + sides[1] + sides[2])
    across = over_zk(piece, 2)
    near = [piece, over_zk(piece, 1)]
    far = [across, over_zk(across, 1)]
    front = assemble(pos, krow, kcol, arrived, front_orig, row_panel, near)
    return (finish(pos, front, row_panel, far), row_panel)


def solution(mesh):
    rows = ("hyp", "x", "z", "core")
    split = Mesh(mesh.devices.reshape(-1, 4, 2, 2, 4), rows + ("col",))
    in_specs = (P(rows, "col"), P(rows, "col"), P("hyp", None), P("hyp", None))
    out_specs = (P(rows, "col"), P(rows, None))
    return jax.shard_map(local, mesh=split, in_specs=in_specs, out_specs=out_specs, check_vma=False)
```

```python
import jax
import jax.numpy as jnp
from jax import lax
from jax.experimental import pallas as pl
from jax.experimental.pallas import tpu as pltpu
from jax.sharding import Mesh, PartitionSpec as P


SMEM = pltpu.MemorySpace.SMEM
VMEM = pltpu.MemorySpace.VMEM
CB = 64
MB = 5
QB = 20
FB = 80
CHUNKS = ((0, 0, 1), (0, 1, 2), (1, 0, 2))
PLACES = [(x, z, core) for x in range(4) for z in range(2) for core in range(2)]


def params(mib):
    return pltpu.CompilerParams(vmem_limit_bytes=mib << 20)


def tables_kernel(map_ref, pos_ref, sel_ref, jsel_ref, jl_ref, krow_ref, kcol_ref, inv_ref, cnt_ref):
    row = pos_ref[0]
    col = pos_ref[1]
    x = row // 4
    zk = row % 4
    child = row // 8
    group = (row % 8) // 2

    def clear(i, _):
        inv_ref[i] = -1
        return 0

    lax.fori_loop(0, 2 * FB, clear, 0, unroll=8)
    for c in range(2):

        def invert(i, _):
            inv_ref[c * FB + map_ref[c, i]] = i
            return 0

        lax.fori_loop(0, CB, invert, 0, unroll=8)
    for y in range(4):

        def pick(q, counts):
            v = inv_ref[child * FB + y * QB + q]
            hit = jnp.logical_and(v >= 0, v // 16 == group)
            sel_ref[jnp.where(hit, y * 4 + counts[0], 16)] = v % 16
            hit_j = jnp.logical_and(v >= 0, v // 16 == col)
            jsel_ref[jnp.where(hit_j, y * 4 + counts[1], 16)] = v % 16
            return counts[0] + hit.astype(jnp.int32), counts[1] + hit_j.astype(jnp.int32)

        lax.fori_loop(0, QB, pick, (jnp.int32(0), jnp.int32(0)))
    for c in range(2):
        count = 0
        for p in range(MB):
            hit = inv_ref[c * FB + row * MB + p] >= 0
            krow_ref[c * MB + p] = jnp.where(hit, count, -1)
            count = count + hit.astype(jnp.int32)
        for g in range(10):
            cnt_ref[g] = 0

        def arrive(q, _):
            v = inv_ref[c * FB + col * QB + q]
            hit = v >= 0
            g = jnp.where(hit, v // 16, 4)
            rank = cnt_ref[g]
            cnt_ref[g] = rank + 1
            sender = ((g % 2) * 2 + rank % 2) ^ zk
            kcol_ref[c * QB + q] = jnp.where(hit, ((rank // 2) * 4 + sender) * 4 + c * 2 + g // 2, -1)
            return 0

        lax.fori_loop(0, QB, arrive, 0)
        for d in range(4):

            def pass_on(q, count):
                v = inv_ref[c * FB + x * QB + d * MB + q]
                hit = v >= 0
                g = jnp.where(hit, v // 16, 4)
                slot = cnt_ref[5 + g]
                cnt_ref[5 + g] = slot + 1
                jl_ref[jnp.where(hit, c * 16 + d * 4 + count, 32)] = g * 4 + slot
                return count + hit.astype(jnp.int32)

            lax.fori_loop(0, MB, pass_on, jnp.int32(0))


def tables(child_map, pos):
    shapes = [32, 32, 48, 16, 48]
    return pl.pallas_call(
        tables_kernel,
        out_shape=[jax.ShapeDtypeStruct((n,), jnp.int32) for n in shapes],
        in_specs=[pl.BlockSpec(memory_space=SMEM)] * 2,
        out_specs=[pl.BlockSpec(memory_space=SMEM)] * 5,
        scratch_shapes=[pltpu.SMEM((2 * FB,), jnp.int32), pltpu.SMEM((16,), jnp.int32)],
        compiler_params=params(63),
        name="tables",
    )(child_map, pos)


def pack_first(sel, jsel, pos, own, other, chunk):
    block = own.shape[0] // 8
    turn, first, last = (n * block // 2 if i else n for i, n in enumerate(CHUNKS[chunk]))

    def kernel(sel_ref, jsel_ref, pos_ref, own_ref, other_ref, out_ref, sem):
        core = pos_ref[0] % 2
        for y in range(4):
            index = sel_ref[y * 4 + 2 * turn + core]
            rows = pl.ds(pl.multiple_of((index % 8) * block + first, block // 2), last - first)
            mine = index // 8 == core

            def copy(ref):
                for x in range(4):
                    for k in range(4):
                        cols = pl.ds(pl.multiple_of(jsel_ref[x * 4 + k] * block, block), block)
                        pltpu.make_async_copy(
                            ref.at[rows, cols],
                            out_ref.at[x * 4 + y, :, pl.ds(k * block, block)],
                            sem,
                        ).start()

            pl.when(mine)(lambda: copy(own_ref))
            pl.when(jnp.logical_not(mine))(lambda: copy(other_ref))

        pltpu.make_async_copy(out_ref, out_ref, sem).wait()

    return pl.pallas_call(
        kernel,
        out_shape=jax.ShapeDtypeStruct((16, last - first, 4 * block), own.dtype),
        in_specs=[pl.BlockSpec(memory_space=SMEM)] * 3 + [pl.BlockSpec(memory_space=pltpu.MemorySpace.HBM)] * 2,
        out_specs=pl.BlockSpec(memory_space=VMEM),
        scratch_shapes=[pltpu.SemaphoreType.DMA(())],
        compiler_params=params(63),
    )(sel, jsel, pos, own, other)


def pack_second(jl, pos, arrived):
    block = arrived.shape[2] // 4

    def kernel(jl_ref, pos_ref, in_ref, *out_refs):
        zk = pos_ref[0] % 4
        for d in range(4):
            for xs in range(4):
                for k in range(4):
                    code = jl_ref[(xs // 2) * 16 + (zk ^ d) * 4 + k]
                    cols = pl.ds(pl.multiple_of((code % 4) * block, block), block)
                    out_refs[min(d, 2)][xs + 4 * (d == 3), :, k * block : (k + 1) * block] = in_ref[
                        xs * 4 + code // 4, :, cols
                    ]

    return pl.pallas_call(
        kernel,
        out_shape=[
            jax.ShapeDtypeStruct((n,) + arrived.shape[1:], arrived.dtype) for n in (4, 4, 8)
        ],
        in_specs=[pl.BlockSpec(memory_space=SMEM)] * 2 + [pl.BlockSpec(memory_space=VMEM)],
        out_specs=[pl.BlockSpec(memory_space=VMEM)] * 3,
        compiler_params=params(63),
    )(jl, pos, arrived)


def fill_eyes(eye_ref):
    block = eye_ref.shape[1]
    i = lax.broadcasted_iota(jnp.int32, (block, block), 0)
    j = lax.broadcasted_iota(jnp.int32, (block, block), 1)
    eye = (i == j).astype(jnp.float32).astype(jnp.bfloat16)
    zero = jnp.zeros((block, block), jnp.bfloat16)
    for v in range(4):
        eye_ref[v, :, :block] = eye if v & 1 else zero
        eye_ref[v, :, block:] = eye if v & 2 else zero


def front_tile(orig, buf_ref, krow_ref, kcol_ref, eye_ref, p, q):
    block = orig.shape[0]
    parts = []
    bits = 0
    for c in range(2):
        k = krow_ref[c * MB + p]
        e = kcol_ref[c * QB + q]
        bits = bits + jnp.where(jnp.logical_and(k >= 0, e >= 0), 1 << c, 0)
        start = pl.multiple_of(jnp.maximum(k, 0) * block, block)
        parts.append(buf_ref[jnp.maximum(e, 0), :, pl.ds(start, block)])
    both = jnp.concatenate(parts, axis=1)
    added = lax.dot_general(
        eye_ref[bits], both, (((1,), (1,)), ((), ())), preferred_element_type=jnp.float32
    )
    return (orig.astype(jnp.float32) + added).astype(jnp.bfloat16)


def gather(refs, buf_ref, sem, meanwhile):
    half = buf_ref.shape[1] // 2
    copies = []
    for n, ref in enumerate(refs):
        turn, first, last = CHUNKS[n // 4]
        d = n % 4
        source = ref.at[pl.ds(4, 4)] if d == 3 else ref.at[pl.ds(0, 4)]
        target = buf_ref.at[pl.ds(turn * 16 + d * 4, 4), pl.ds(first * half, (last - first) * half)]
        copies.append(pltpu.make_async_copy(source, target, sem.at[n]))
    for copy in copies:
        copy.start()
    meanwhile()
    for copy in copies:
        copy.wait()


def strip_panel(krow, kcol, arrived, front_orig, panel_inverse):
    block = arrived[0].shape[2] // 4
    rows = front_orig.shape[0]

    def kernel(krow_ref, kcol_ref, *refs):
        orig_ref, inverse_ref, out_ref, buf_ref, eye_ref, sem = refs[8:]
        gather(refs[:8], buf_ref, sem, lambda: fill_eyes(eye_ref))
        for p in range(MB):
            here = slice(p * block, (p + 1) * block)
            tiles = [
                front_tile(
                    orig_ref[here, q * block : (q + 1) * block],
                    buf_ref, krow_ref, kcol_ref, eye_ref, p, q,
                )
                for q in range(2)
            ]
            out_ref[here, :] = jnp.dot(
                jnp.concatenate(tiles, axis=1), inverse_ref[...], preferred_element_type=jnp.float32
            ).astype(jnp.bfloat16)

    return pl.pallas_call(
        kernel,
        grid=(1,),
        out_shape=jax.ShapeDtypeStruct((rows, 2 * block), jnp.bfloat16),
        in_specs=[pl.BlockSpec(memory_space=SMEM)] * 2
        + [pl.BlockSpec(memory_space=pl.ANY)] * 8
        + [
            pl.BlockSpec((rows, 2 * block), lambda i: (0, 0)),
            pl.BlockSpec(memory_space=VMEM),
        ],
        out_specs=pl.BlockSpec(memory_space=VMEM),
        scratch_shapes=[
            pltpu.VMEM((16, block, 4 * block), jnp.bfloat16),
            pltpu.VMEM((4, block, 2 * block), jnp.bfloat16),
            pltpu.SemaphoreType.DMA((8,)),
        ],
        compiler_params=params(63),
        name="strip_panel",
    )(krow, kcol, *arrived, front_orig, panel_inverse)


def assemble(krow, kcol, arrived, front_orig):
    block = arrived[0].shape[2] // 4
    rows, cols = front_orig.shape

    def kernel(krow_ref, kcol_ref, *refs):
        orig_ref, out_ref, buf_ref, eye_ref, sem = refs[12:]
        step = pl.program_id(0)

        @pl.when(step == 0)
        def _():
            gather(refs[:12], buf_ref, sem, lambda: fill_eyes(eye_ref))

        for q in range(QB // 4):
            side = slice(q * block, (q + 1) * block)
            for p in range(MB):
                here = slice(p * block, (p + 1) * block)
                out_ref[here, side] = front_tile(
                    orig_ref[here, side], buf_ref, krow_ref, kcol_ref, eye_ref, p, step * (QB // 4) + q
                )

    return pl.pallas_call(
        kernel,
        grid=(4,),
        out_shape=jax.ShapeDtypeStruct(front_orig.shape, jnp.bfloat16),
        in_specs=[pl.BlockSpec(memory_space=SMEM)] * 2
        + [pl.BlockSpec(memory_space=pl.ANY)] * 12
        + [pl.BlockSpec((rows, cols // 4), lambda i: (0, i))],
        out_specs=pl.BlockSpec((rows, cols // 4), lambda i: (0, i)),
        scratch_shapes=[
            pltpu.VMEM((32, block, 4 * block), jnp.bfloat16),
            pltpu.VMEM((4, block, 2 * block), jnp.bfloat16),
            pltpu.SemaphoreType.DMA((12,)),
        ],
        compiler_params=params(63),
        name="assemble",
    )(krow, kcol, *arrived, front_orig)


def finish(pos, front, row_panel, pieces):
    _, cols = front.shape
    wide = cols // 4

    def kernel(pos_ref, front_ref, row_ref, p0, p1, p2, p3, out_ref):
        zk = pos_ref[0] % 4
        for w, ref in enumerate((p0, p1, p2, p3)):
            here = pl.ds(pl.multiple_of((zk ^ w) * wide, wide), wide)
            update = lax.dot_general(
                row_ref[...], ref[...], (((1,), (1,)), ((), ())), preferred_element_type=jnp.float32
            )
            out_ref[:, here] = (front_ref[:, here].astype(jnp.float32) - update).astype(jnp.bfloat16)

    return pl.pallas_call(
        kernel,
        out_shape=jax.ShapeDtypeStruct(front.shape, jnp.bfloat16),
        in_specs=[pl.BlockSpec(memory_space=SMEM)] + [pl.BlockSpec(memory_space=VMEM)] * 6,
        out_specs=pl.BlockSpec(memory_space=VMEM),
        compiler_params=params(63),
        name="finish",
    )(pos, front, row_panel, *pieces)


def device(x, z, core, y):
    return ((x * 2 + z) * 2 + core) * 4 + y


def moved(array, pairs):
    return lax.ppermute(array, ("x", "z", "core", "col"), pairs)


def over_zk(array, d):
    return lax.ppermute(array, ("z", "core"), [(r, r ^ d) for r in range(4)])


def local(front_orig, child_updates, child_map, panel_inverse):
    me_x = lax.axis_index("x")
    me_z = lax.axis_index("z")
    me_core = lax.axis_index("core")
    me_col = lax.axis_index("col")
    pos = jnp.stack([me_x * 4 + me_z * 2 + me_core, me_col]).astype(jnp.int32)
    other = over_zk(child_updates, 1)
    sel, jsel, jl, krow, kcol = tables(child_map, pos)

    arrived = []
    for chunk in range(len(CHUNKS)):
        sent = pack_first(sel, jsel, pos, child_updates, other, chunk)
        part = lax.all_to_all(sent, ("x", "col"), 0, 0, tiled=True)
        stay, swap, out = pack_second(jl, pos, part)
        crossed = over_zk(out, 2)
        near = over_zk(swap, 1)
        arrived += [stay, near, crossed, over_zk(crossed, 1)]
    first = arrived[:8]

    panel_0 = strip_panel(krow, kcol, first, front_orig, panel_inverse)
    spread = [
        moved(panel_0, [(device(x, z, k, 0), device(x, z, k, y)) for x, z, k in PLACES])
        for y in range(1, 4)
    ]
    sides = [
        moved(panel_0, [(device(x, z, k, 0), device((x + d) % 4, z, k, x)) for x, z, k in PLACES])
        for d in range(1, 4)
    ]
    row_panel = jnp.where(me_col == 0, panel_0, spread[0] + spread[1] + spread[2])
    piece = jnp.where(me_x == me_col, row_panel, sides[0] + sides[1] + sides[2])
    across = over_zk(piece, 2)
    pieces = [piece, over_zk(piece, 1), across, over_zk(across, 1)]

    front = assemble(krow, kcol, arrived, front_orig)
    return (finish(pos, front, row_panel, pieces), row_panel)


def solution(mesh):
    rows = ("hyp", "x", "z", "core")
    split = Mesh(mesh.devices.reshape(-1, 4, 2, 2, 4), rows + ("col",))
    in_specs = (P(rows, "col"), P(rows, "col"), P("hyp", None), P("hyp", None))
    out_specs = (P(rows, "col"), P(rows, None))
    return jax.shard_map(local, mesh=split, in_specs=in_specs, out_specs=out_specs, check_vma=False)
```
